128 devices in a mesh: field: 16 (over x, z), dom: 8 (over y, core).
Axes of the slice: x: 4, y: 4, z: 4, core: 2. Of those that a mesh axis runs over, the one named last changes fastest.
Arguments:
- coefficients: float32 [512, 128], P('dom'), may hold values from -6 to 6
- copies: int32 [512], P('dom'), may hold values from 1 to 4
- owner: int32 [512, 1], P('dom'), may hold values from 0 to 7; in each aligned block of 64 rows (0 to 63, 64 to 127, ...) at most 16 rows name the same one
- snapshots: int32 [8], replicated, may hold values from 0 to 511
- basis: bfloat16 [4194304, 128], P(('field', 'dom')), may hold values from -3 to 3
- observed: float32 [4194304], P(('field', 'dom')), may hold values from -6 to 6
- precision: float32 [4194304], P(('field', 'dom')), may hold values from 1 to 16
Outputs:
- new_coefficients: float32 [8, 8, 16, 128], P('dom')
The draws below stay inside these ranges and needn't reach their ends.
Inputs may be any that keep to these rules, and one draw needn't show every extreme that they name: Among the 64 particles of one index of dom, at most 16 name the same owner, and in every draw some owner is named by exactly 16 particles of some index of dom.
All inputs are finite; a program needn't handle non-finite values.
Results may differ from the reference program's by a relative error of at most 0.00074.
Values sent between devices are 32-bit elements; how exact they have to be, the bound alone decides.
No kernel may reach another device: no remote copies, remote signals or barrier semaphores. Data moves between devices by JAX's collectives and lax.ppermute only.
A program may use at most 64 MiB of HBM per device.

```python
import math
import jax
import jax.numpy as jnp
import numpy as np
from jax import lax

PTS = 4194304
R = 128
NP_DEV = 64
SNAP = 8
NPART = 512
CAP = 16
N_DOM = 8


def basis_values(key):
    normals = jax.random.truncated_normal(jax.random.fold_in(key, 11), -4.0, 4.0, (PTS, R), jnp.float32)
    blended = normals + 0.5 * jnp.roll(normals, 1, axis=1) + 0.3 * jnp.roll(normals, 5, axis=1)
    column_group = jax.random.permutation(jax.random.fold_in(key, 13), R) % 4
    row_group = jnp.arange(PTS, dtype=jnp.int32) % 4
    weighting = jnp.where(row_group[:, None] == column_group[None, :], 1.0, 0.4)
    column_scales = jnp.exp(jax.random.uniform(jax.random.fold_in(key, 17), (R,), jnp.float32, -1.0, 1.0))
    column_scales = column_scales / jnp.sqrt(jnp.mean(column_scales * column_scales))
    values = blended * weighting * column_scales[None, :] / math.sqrt(0.33 * R)
    return jnp.clip(values, -3.0, 3.0)


def draw_basis(key, part):
    return basis_values(key).astype(jnp.bfloat16)


def draw_observed(key, part):
    values = basis_values(key)
    truth_vector = 0.7 * jax.random.normal(jax.random.fold_in(key, 19), (R,), jnp.float32)
    noise_part = 0.5 * jax.random.normal(jax.random.fold_in(key, 23), (PTS,), jnp.float32)
    signal = jnp.dot(values, truth_vector, precision=lax.Precision.HIGHEST)
    return jnp.clip(signal + noise_part, -6.0, 6.0)


def with_ends(values, key, low, top_value):
    longest = values.shape.index(max(values.shape))
    spots = []
    for shift in (0, 1):
        where = [jax.random.randint(jax.random.fold_in(key, axis), (), 0, length) for axis, length in enumerate(values.shape)]
        where[longest] = (where[longest] + shift) % values.shape[longest]
        spots.append(tuple(where))
    return values.at[spots[0]].set(low).at[spots[1]].set(top_value)


def level_of(own_key, shape, split, smallest, high):
    def one(dim, parts):
        heights = jax.random.uniform(jax.random.fold_in(jax.random.fold_in(own_key, 6), dim), (parts,), jnp.float32, smallest / len(split), high / len(split))
        return jnp.repeat(jnp.exp(heights), shape[dim] // parts).reshape((-1,) + (1,) * (len(shape) - dim - 1))

    factor_of = one(*split[0])
    for cut in split[1:]:
        factor_of = factor_of * one(*cut)
    return factor_of


def shared_out(own_key, own, number, rows, number_of, top, reach, skew):
    order = jax.random.permutation(own_key, number_of)
    heavy_load, usual = load_shares(number_of, rows * top, reach, skew, True), load_shares(number_of, rows * top, reach, skew, False)
    places = jnp.arange(number_of)

    def named(tallies, turn):
        used = int((tallies > 0).sum())
        fixed = max(1, used // 4)
        moved = fixed + (places - fixed + turn * (used - fixed)) % max(1, number_of - fixed)
        return jnp.zeros((number_of,), jnp.int32).at[order[jnp.where(places < fixed, places, moved)]].set(jnp.asarray(tallies, jnp.int32))

    tallies = jnp.where(number % 4 == 0, named(heavy_load, number // 4), named(usual, number - number // 4 - 1))
    mixed = jax.random.permutation(jax.random.fold_in(own, 3), number_of)
    giver, receiver = mixed[0:number_of // 2 * 2:2], mixed[1:number_of // 2 * 2:2]
    slack = jnp.minimum(tallies[giver] - 1, reach - tallies[receiver]) // 2
    slack = jnp.where((giver == order[0]) | (receiver == order[0]) | (tallies[receiver] == 0), 0, jnp.maximum(slack, 0))
    moved = jax.random.randint(jax.random.fold_in(own, 4), (number_of // 2,), 0, 1 << 20) % (slack + 1)
    tallies = tallies.at[giver].add(-moved).at[receiver].add(moved)
    labels = jnp.searchsorted(jnp.cumsum(tallies), jnp.arange(rows * top), side="right").astype(jnp.int32)
    table = labels.reshape(top, rows).T
    table = table[jax.random.permutation(jax.random.fold_in(own, 1), rows)]
    turn = jax.random.randint(jax.random.fold_in(own, 2), (rows, 1), 0, top)
    return jnp.take_along_axis(table, (jnp.arange(top)[None, :] + turn) % top, axis=1)


def load_shares(amount, total, bound, skew, full):
    portions = [(1 << 20) // math.isqrt(grade ** skew) + 1 for grade in range(1, amount + 1)]
    largest = bound if full else min(bound, max(-(-total // amount), total * portions[0] // sum(portions)))
    least = 1 if total - largest >= amount - 1 else 0
    given, spare = [largest] + [least] * (amount - 1), total - largest - least * (amount - 1)
    while spare > 0:
        movable = [i for i in range(1, amount) if given[i] < largest] or [i for i in range(1, amount) if given[i] < bound]
        mass, left = sum([portions[i] for i in movable]), spare
        for i in movable:
            more = min(bound - given[i], max(1, left * portions[i] // mass), spare)
            given[i] = given[i] + more
            spare = spare - more
    return np.array(given)


def gaussian(rng, dims, scale, bound, split=(), kind=jnp.bfloat16):
    level = level_of(rng, dims, split, -0.22, 0.18) if split else 1.0
    entries = jax.random.normal(rng, dims, jnp.float32) * scale * level
    return jnp.minimum(jnp.maximum(entries, -bound), bound).astype(kind)


def setup_inputs(seed: int = 0) -> dict:
    streams_of = jax.random.split(jax.random.key(seed), 8)
    coefficients = gaussian(streams_of[0], (NPART, R), 1.0, 6.0, ((0, 8),), jnp.float32)
    copies = with_ends(jax.random.randint(streams_of[1], (NPART,), 1, 5), jax.random.fold_in(streams_of[1], 1), 1, 4).astype(jnp.int32)
    owner_keys = jax.random.split(jax.random.fold_in(streams_of[2], 1), NPART // NP_DEV)
    owner_turns = jax.random.permutation(jax.random.fold_in(streams_of[2], 3), NPART // NP_DEV)
    owner = jax.vmap(lambda own, number: shared_out(jax.random.fold_in(streams_of[2], 2), own, number, NP_DEV, N_DOM, 1, CAP, 2))(owner_keys, owner_turns).reshape((NPART, 1))
    snapshots = with_ends(jax.random.randint(streams_of[3], (SNAP,), 0, NPART), jax.random.fold_in(streams_of[3], 1), 0, NPART - 1).astype(jnp.int32)
    basis = draw_basis(jax.random.fold_in(streams_of[7], 71), 0)
    observed = draw_observed(jax.random.fold_in(streams_of[7], 71), 0)
    precision = jnp.clip(jnp.exp(math.log(16.0) - 2.7725887 * jax.random.uniform(streams_of[6], (PTS,), jnp.float32) ** level_of(streams_of[6], (PTS,), ((0, 128),), -0.2, 0.2)), 1.0, 16.0)
    return {"coefficients": coefficients, "copies": copies, "owner": owner, "snapshots": snapshots, "basis": basis, "observed": observed, "precision": precision}


highest = lax.Precision.HIGHEST

def reference(coefficients, copies, owner, snapshots, basis, observed, precision):
    density = R / PTS
    rounded = coefficients.astype(jnp.bfloat16)
    picked = rounded[snapshots]
    block_width = math.gcd(PTS, 16384)
    last_pair = (((1,), (1,)), ((), ()))

    def point_block(sums_carry, block_index):
        grad_sum, hess_sum = sums_carry
        row_start = block_index * block_width
        basis_rows = lax.dynamic_slice_in_dim(basis, row_start, block_width, 0)
        observed_part = lax.dynamic_slice_in_dim(observed, row_start, block_width, 0)
        precision_part = lax.dynamic_slice_in_dim(precision, row_start, block_width, 0)
        field_values = lax.dot_general(rounded.astype(jnp.float32), basis_rows.astype(jnp.float32), last_pair, preferred_element_type=jnp.float32)
        pulled = (density * precision_part * jnp.tanh(field_values - observed_part)).astype(jnp.bfloat16)
        grad_sum = grad_sum + jnp.dot(pulled.astype(jnp.float32), basis_rows.astype(jnp.float32), preferred_element_type=jnp.float32)
        snap_values = lax.dot_general(picked.astype(jnp.float32), basis_rows.astype(jnp.float32), last_pair, preferred_element_type=jnp.float32)
        slopes = jnp.tanh(snap_values - observed_part)
        bending = density * precision_part * (1.0 - slopes * slopes)
        scaled = (bending[:, :, None] * basis_rows.astype(jnp.float32)[None]).astype(jnp.bfloat16)
        hess_sum = hess_sum + jnp.einsum('spr,pq->srq', scaled.astype(jnp.float32), basis_rows.astype(jnp.float32))
        return ((grad_sum, hess_sum), None)
    start_sums = (jnp.zeros((NPART, R), jnp.float32), jnp.zeros((SNAP, R, R), jnp.float32))
    (grad_sum, hess_sum), _ = lax.scan(point_block, start_sums, jnp.arange(PTS // block_width, dtype=jnp.int32))
    hessians = jnp.eye(R, dtype=jnp.float32)[None] + hess_sum
    mean_hess = jnp.mean(hessians, axis=0)
    hess_trace = jnp.trace(mean_hess)
    repulse = 6.0 / hess_trace
    lifted = jnp.dot(coefficients, mean_hess, precision=highest)
    quad_norms = jnp.sum(lifted * coefficients, axis=1)
    cross_terms = lax.dot_general(lifted.astype(jnp.float32), coefficients.astype(jnp.float32), last_pair, precision=highest, preferred_element_type=jnp.float32)
    distance = quad_norms[:, None] + quad_norms[None, :] - 2.0 * cross_terms
    weights = copies.astype(jnp.float32)[None, :] * jnp.exp(-3.0 * distance / hess_trace)
    weight_total = jnp.sum(weights, axis=1)
    weights_low = weights.astype(jnp.bfloat16)
    carried_low = (coefficients + repulse * lifted).astype(jnp.bfloat16)
    numerator = jnp.dot(weights_low.astype(jnp.float32), carried_low.astype(jnp.float32), preferred_element_type=jnp.float32)
    numerator = numerator + jnp.dot(weights_low.astype(jnp.float32), grad_sum, precision=highest)
    drift_rows = -numerator / weight_total[:, None] + repulse * lifted
    snap_coef = coefficients[snapshots]
    snap_cross = lax.dot_general(lifted.astype(jnp.float32), snap_coef.astype(jnp.float32), last_pair, precision=highest, preferred_element_type=jnp.float32)
    snap_dist = quad_norms[:, None] + quad_norms[snapshots][None, :] - 2.0 * snap_cross
    mixture = 1.0 / jnp.square(1.0 + snap_dist / hess_trace)
    mixture = mixture / jnp.sum(mixture, axis=1, keepdims=True)
    local_hess = jnp.einsum('is,srq->irq', mixture, hessians, precision=highest)
    factor = jnp.linalg.cholesky(local_hess)
    halfway = jax.scipy.linalg.solve_triangular(factor, drift_rows[:, :, None], lower=True)
    newton_step = jax.scipy.linalg.solve_triangular(factor, halfway, lower=True, trans=1)
    updated = coefficients + newton_step[:, :, 0]

    def pack_block(block_moved, block_owner):
        onehot = (block_owner[:, None] == jnp.arange(N_DOM, dtype=jnp.int32)[None, :]).astype(jnp.int32)
        before = jnp.sum(onehot * (jnp.cumsum(onehot, axis=0) - 1), axis=1)
        target = block_owner * CAP + before
        placing = (jnp.arange(N_DOM * CAP, dtype=jnp.int32)[:, None] == target[None, :]).astype(jnp.float32)
        return jnp.dot(placing, block_moved, precision=highest).reshape(N_DOM, CAP, R)
    packed = jax.vmap(pack_block)(updated.reshape(N_DOM, NP_DEV, R), owner[:, 0].reshape(N_DOM, NP_DEV))
    return jnp.transpose(packed, (1, 0, 2, 3))
```

```python
import functools

import jax
import jax.numpy as jnp
from jax import lax
from jax.experimental import pallas as pl
from jax.experimental.pallas import tpu as pltpu
from jax.sharding import Mesh
from jax.sharding import PartitionSpec as P

PTS = 4194304
R = 128
NP_DEV = 64
NPART = 512
SNAP = 8
N_DOM = 8
ROWS = NPART + SNAP * R
HALF = ROWS // 2
LINES = 72
X, Z, Y, C = "field_0", "field_1", "dom_0", "dom_1"
DOM = (Y, C)
FIELD = (X, Z)
CHIPS = (X, Z, Y)
FIELD_DOM = (X, Z, Y, C)
f32, bf16 = jnp.float32, jnp.bfloat16
highest = lax.Precision.HIGHEST
last_pair = (((1,), (1,)), ((), ()))
VMEM_LIMIT = 60 << 20


def particles(gathered_ref):
    return jnp.concatenate([gathered_ref[d, 0:NP_DEV, :] for d in range(N_DOM)], axis=0)


def points_kernel(block, chunk, picks_ref, core_ref, gathered_ref, obs_ref, prec_ref, basis_ref,
                  keep_ref, send_ref, coef_ref, sums_ref, left_ref, right_ref):
    step = pl.program_id(0)

    @pl.when(step == 0)
    def _():
        sums_ref[...] = jnp.zeros_like(sums_ref)
        coef_ref[0:NPART, :] = particles(gathered_ref).astype(bf16)
        rows = []
        for s in range(SNAP):
            j = picks_ref[s]
            rows.append(gathered_ref[j // NP_DEV, pl.ds(j % NP_DEV, 1), :])
        rows.append(jnp.zeros((SNAP, R), f32))
        coef_ref[NPART : NPART + 16, :] = jnp.concatenate(rows, axis=0).astype(bf16)

    for c in range(block // chunk):
        at = pl.ds(c * chunk, chunk)
        rows = basis_ref[at, :]
        columns = rows.T
        prec = prec_ref[:, at]
        right_ref[at, :] = (columns.astype(f32) * prec).astype(bf16).T
        field = lax.dot_general(coef_ref[...], rows, last_pair, preferred_element_type=f32)
        slopes = jnp.tanh(field[: NPART + SNAP] - obs_ref[:, at])
        left_ref[0:NPART, at] = slopes[:NPART].astype(bf16)
        picked = slopes[NPART : NPART + SNAP]
        bend = 1.0 - picked * picked
        for s in range(SNAP):
            top = NPART + s * R
            left_ref[top : top + R, at] = bend[s : s + 1, :].astype(bf16) * columns
    sums_ref[...] += jnp.dot(left_ref[...], right_ref[...], preferred_element_type=f32)

    @pl.when(step == pl.num_programs(0) - 1)
    def _():
        for core in range(2):

            @pl.when(core_ref[0] == core)
            def _():
                keep_ref[...] = sums_ref[core * HALF : (core + 1) * HALF, :]
                send_ref[...] = sums_ref[(1 - core) * HALF : (2 - core) * HALF, :]


def points_pass(snapshots, core, gathered, observed, precision, basis):
    block, chunk = 2048, 256
    count = basis.shape[0]
    whole = lambda i, *_: (0, 0)
    return pl.pallas_call(
        functools.partial(points_kernel, block, chunk),
        out_shape=[jax.ShapeDtypeStruct((HALF, R), f32)] * 2,
        grid_spec=pltpu.PrefetchScalarGridSpec(
            num_scalar_prefetch=2,
            grid=(count // block,),
            in_specs=[
                pl.BlockSpec((N_DOM, LINES, R), lambda i, *_: (0, 0, 0)),
                pl.BlockSpec((1, block), lambda i, *_: (0, i)),
                pl.BlockSpec((1, block), lambda i, *_: (0, i)),
                pl.BlockSpec((block, R), lambda i, *_: (i, 0)),
            ],
            out_specs=[pl.BlockSpec((HALF, R), whole)] * 2,
            scratch_shapes=[
                pltpu.VMEM((NPART + 16, R), bf16),
                pltpu.VMEM((ROWS, R), f32),
                pltpu.VMEM((ROWS, block), bf16),
                pltpu.VMEM((block, R), bf16),
            ],
        ),
        compiler_params=pltpu.CompilerParams(vmem_limit_bytes=VMEM_LIMIT),
        name="points_pass",
    )(snapshots, core, gathered, observed.reshape(1, count), precision.reshape(1, count), basis)


def lane_of(rows, k):
    return jnp.take_along_axis(rows, jnp.full(rows.shape, k, jnp.int32), axis=1)


def steps_kernel(where_ref, picks_ref, gathered_ref, mine_ref, other_ref, out_ref,
                 sums_ref, sys_ref):
    scale = R / PTS
    core, dom, source, first = where_ref[0], where_ref[1], where_ref[2], where_ref[3]
    for half in range(2):

        @pl.when(core == half)
        def _():
            sums_ref[half * HALF : (half + 1) * HALF, :] = mine_ref[...]
            sums_ref[(1 - half) * HALF : (2 - half) * HALF, :] = other_ref[...]

    lane = lax.broadcasted_iota(jnp.int32, (8, R), 1)
    sub = lax.broadcasted_iota(jnp.int32, (8, R), 0)
    square_r = lax.broadcasted_iota(jnp.int32, (R, R), 0)
    square_q = lax.broadcasted_iota(jnp.int32, (R, R), 1)
    eye = (square_r == square_q).astype(f32)

    everyone = particles(gathered_ref)
    tags = [gathered_ref[d, NP_DEV : NP_DEV + 1, :] for d in range(N_DOM)]
    low = lane[0:1] < NP_DEV
    counts = jnp.concatenate(
        [jnp.where(low, tags[d], pltpu.roll(tags[d + 1], NP_DEV, 1)) for d in range(0, N_DOM, 2)], axis=1
    )

    owners = pltpu.roll(jnp.broadcast_to(gathered_ref[source, NP_DEV : NP_DEV + 1, :], (8, R)), NP_DEV, 1)
    named = jnp.where((owners == dom.astype(f32)) & (lane < NP_DEV), 1.0, 0.0)
    before = jnp.dot(named, (square_r < square_q).astype(f32), precision=highest, preferred_element_type=f32)
    slot = (sub + first).astype(f32)
    choose = jnp.where((named > 0.5) & (before == slot), 1.0, 0.0)
    valid = jnp.sum(choose, axis=1, keepdims=True)
    own = jnp.dot(choose[:, :NP_DEV], gathered_ref[source, 0:NP_DEV, :], precision=highest,
                  preferred_element_type=f32)

    mean_hess = sums_ref[NPART : NPART + R, :]
    for s in range(1, SNAP):
        mean_hess = mean_hess + sums_ref[NPART + s * R : NPART + (s + 1) * R, :]
    mean_hess = eye + mean_hess * (scale / SNAP)
    trace = jnp.sum(jnp.sum(mean_hess * eye, axis=1, keepdims=True), axis=0, keepdims=True)
    repulse = 6.0 / trace

    lifted = jnp.dot(everyone, mean_hess, precision=highest, preferred_element_type=f32)
    ones = jnp.ones((8, R), f32)
    norms = lax.dot_general(ones, lifted * everyone, last_pair, precision=highest, preferred_element_type=f32)
    own_lift = jnp.dot(own, mean_hess, precision=highest, preferred_element_type=f32)
    own_norm = jnp.sum(own_lift * own, axis=1, keepdims=True)
    cross = lax.dot_general(own_lift, everyone, last_pair, precision=highest, preferred_element_type=f32)
    distance = own_norm + norms - 2.0 * cross
    weights = counts * jnp.exp(-3.0 * distance / trace)
    total = jnp.sum(weights, axis=1, keepdims=True)
    low_weights = weights.astype(bf16)
    carried = (everyone + repulse * lifted).astype(bf16)
    numerator = jnp.dot(low_weights, carried, preferred_element_type=f32)
    grad = jnp.dot(low_weights.astype(f32), sums_ref[0:NPART, :], precision=highest, preferred_element_type=f32)
    drift = -(numerator + scale * grad) / total + repulse * own_lift

    rows = []
    for s in range(SNAP):
        j = picks_ref[s]
        rows.append(gathered_ref[j // NP_DEV, pl.ds(j % NP_DEV, 1), :])
    rows.append(jnp.zeros((R - SNAP, R), f32))
    picked = jnp.concatenate(rows, axis=0)
    picked_lift = jnp.dot(picked, mean_hess, precision=highest, preferred_element_type=f32)
    picked_norm = lax.dot_general(ones, picked_lift * picked, last_pair, precision=highest,
                                  preferred_element_type=f32)
    picked_cross = lax.dot_general(own_lift, picked, last_pair, precision=highest, preferred_element_type=f32)
    apart = 1.0 + (own_norm + picked_norm - 2.0 * picked_cross) / trace
    mixture = jnp.where(lane < SNAP, 1.0 / (apart * apart), 0.0)
    mixture = mixture / jnp.sum(mixture, axis=1, keepdims=True)

    shares = [jnp.broadcast_to(mixture[:, s : s + 1], (8, R)) for s in range(SNAP)]
    share_sum = functools.reduce(jnp.add, shares)
    shares = [share * scale for share in shares]

    def assemble(g, carry):
        tiles = [sums_ref[pl.ds(pl.multiple_of(NPART + s * R + g * 8, 8), 8), :] for s in range(SNAP)]
        for k in range(8):
            row = jnp.where(lane == g * 8 + k, share_sum, 0.0)
            for s in range(SNAP):
                row = row + shares[s] * tiles[s][k : k + 1, :]
            sys_ref[g * 8 + k] = row
        return carry

    lax.fori_loop(0, R // 8, assemble, 0)

    def eliminate(start, h, carry):
        rhs, inverses = carry
        k = start + 2 * h
        r0 = sys_ref[k]
        i0 = 1.0 / lane_of(r0, k)
        s0 = jnp.where(lane > k, r0, 0.0) * i0
        r1 = sys_ref[k + 1] - lane_of(r0, k + 1) * s0
        sys_ref[k + 1] = r1
        i1 = 1.0 / lane_of(r1, k + 1)
        m0 = jnp.where(lane > k + 1, r0, 0.0)
        m1 = jnp.where(lane > k + 1, r1, 0.0)
        s1 = m1 * i1
        rhs = rhs - lane_of(rhs, k) * s0
        rhs = rhs - lane_of(rhs, k + 1) * s1
        inverses = jnp.where(lane == k, i0, jnp.where(lane == k + 1, i1, inverses))
        for i in range(start, R):
            sys_ref[i] = sys_ref[i] - m0[:, i : i + 1] * s0 - m1[:, i : i + 1] * s1
        return rhs, inverses

    carry = (drift, jnp.zeros((8, R), f32))
    segment = R // 4
    for start in range(0, R, segment):
        carry = lax.fori_loop(0, segment // 2, functools.partial(eliminate, start), carry)
    rhs, inverses = carry

    def substitute(n, rhs):
        m = R - 1 - n
        x = lane_of(rhs * inverses, m)
        return rhs - jnp.where(lane < m, sys_ref[m], 0.0) * x

    rhs = lax.fori_loop(0, R, substitute, rhs, unroll=8)
    out_ref[...] = jnp.where(valid > 0.5, own + rhs * inverses, 0.0)


def newton_rows(where, snapshots, gathered, mine, other):
    vmem = pl.BlockSpec(memory_space=pltpu.VMEM)
    smem = pl.BlockSpec(memory_space=pltpu.SMEM)
    return pl.pallas_call(
        steps_kernel,
        out_shape=jax.ShapeDtypeStruct((8, R), f32),
        in_specs=[smem, smem, vmem, vmem, vmem],
        out_specs=vmem,
        scratch_shapes=[pltpu.VMEM((ROWS, R), f32), pltpu.VMEM((R, 8, R), f32)],
        compiler_params=pltpu.CompilerParams(vmem_limit_bytes=VMEM_LIMIT),
        name="newton_rows",
    )(where, snapshots, gathered, mine, other)


def sent_to_all(shard, axes):
    copies = jnp.broadcast_to(shard, (lax.axis_size(axes), *shard.shape))
    return lax.all_to_all(copies, axes, split_axis=0, concat_axis=0, tiled=True)


def body(coefficients, copies, owner, snapshots, basis, observed, precision):
    tags = jnp.concatenate([copies, owner[:, 0]]).astype(f32)[None]
    lines = jnp.concatenate([coefficients, tags, jnp.zeros((LINES - NP_DEV - 1, R), f32)], axis=0)
    gathered = sent_to_all(lines, DOM)
    core = lax.axis_index(C)
    swap = [(0, 1), (1, 0)]
    keep, send = points_pass(snapshots, core.reshape(1), gathered, observed, precision, basis)
    part = keep + lax.ppermute(send, C, swap)
    chips = lax.axis_size(CHIPS)
    blocks = lax.all_to_all(part.reshape(chips, HALF // chips, R), CHIPS, 0, 0, tiled=True)
    mine = sent_to_all(jnp.sum(blocks, axis=0), CHIPS).reshape(HALF, R)
    other = lax.ppermute(mine, C, swap)
    seat = lax.axis_index(FIELD)
    where = jnp.stack([core, lax.axis_index(DOM), seat // 2, seat % 2 * 8])
    rows = newton_rows(where, snapshots, gathered, mine, other)
    return sent_to_all(rows, FIELD).reshape(1, N_DOM, 16, R)


def solution(mesh):
    finer = Mesh(mesh.devices.reshape(4, 4, 4, 2), FIELD_DOM)
    return jax.shard_map(
        body,
        mesh=finer,
        in_specs=(
            P(DOM, None),
            P(DOM),
            P(DOM, None),
            P(),
            P(FIELD_DOM, None),
            P(FIELD_DOM),
            P(FIELD_DOM),
        ),
        out_specs=P(DOM, None, None, None),
        check_vma=False,
    )
```

```python
import functools

import jax
import jax.numpy as jnp
from jax import lax
from jax.experimental import pallas as pl
from jax.experimental.pallas import tpu as pltpu
from jax.sharding import Mesh
from jax.sharding import PartitionSpec as P

PTS = 4194304
R = 128
NP_DEV = 64
NPART = 512
SNAP = 8
N_DOM = 8
ROWS = NPART + SNAP * R
HALF = ROWS // 2
LINES = 72
X, Z, Y, C = "field_0", "field_1", "dom_0", "dom_1"
DOM = (Y, C)
FIELD = (X, Z)
CHIPS = (X, Z, Y)
FIELD_DOM = (X, Z, Y, C)
f32, bf16 = jnp.float32, jnp.bfloat16
highest = lax.Precision.HIGHEST
last_pair = (((1,), (1,)), ((), ()))
VMEM_LIMIT = 60 << 20


def particles(gathered_ref):
    return jnp.concatenate([gathered_ref[d, 0:NP_DEV, :] for d in range(N_DOM)], axis=0)


def points_kernel(block, chunk, picks_ref, core_ref, gathered_ref, obs_ref, prec_ref, basis_ref,
                  keep_ref, send_ref, coef_ref, sums_ref, left_ref, right_ref):
    step = pl.program_id(0)

    @pl.when(step == 0)
    def _():
        sums_ref[...] = jnp.zeros_like(sums_ref)
        coef_ref[0:NPART, :] = particles(gathered_ref).astype(bf16)
        rows = []
        for s in range(SNAP):
            j = picks_ref[s]
            rows.append(gathered_ref[j // NP_DEV, pl.ds(j % NP_DEV, 1), :])
        rows.append(jnp.zeros((SNAP, R), f32))
        coef_ref[NPART : NPART + 16, :] = jnp.concatenate(rows, axis=0).astype(bf16)

    for c in range(block // chunk):
        at = pl.ds(c * chunk, chunk)
        rows = basis_ref[at, :]
        columns = rows.T
        prec = prec_ref[:, at]
        right_ref[at, :] = (columns.astype(f32) * prec).astype(bf16).T
        field = lax.dot_general(coef_ref[...], rows, last_pair, preferred_element_type=f32)
        slopes = jnp.tanh(field[: NPART + SNAP] - obs_ref[:, at])
        left_ref[0:NPART, at] = slopes[:NPART].astype(bf16)
        picked = slopes[NPART : NPART + SNAP]
        bend = 1.0 - picked * picked
        for s in range(SNAP):
            top = NPART + s * R
            left_ref[top : top + R, at] = bend[s : s + 1, :].astype(bf16) * columns
    sums_ref[...] += jnp.dot(left_ref[...], right_ref[...], preferred_element_type=f32)

    @pl.when(step == pl.num_programs(0) - 1)
    def _():
        for core in range(2):

            @pl.when(core_ref[0] == core)
            def _():
                keep_ref[...] = sums_ref[core * HALF : (core + 1) * HALF, :]
                send_ref[...] = sums_ref[(1 - core) * HALF : (2 - core) * HALF, :]


def points_pass(snapshots, core, gathered, observed, precision, basis):
    block, chunk = 2048, 256
    count = basis.shape[0]
    whole = lambda i, *_: (0, 0)
    return pl.pallas_call(
        functools.partial(points_kernel, block, chunk),
        out_shape=[jax.ShapeDtypeStruct((HALF, R), f32)] * 2,
        grid_spec=pltpu.PrefetchScalarGridSpec(
            num_scalar_prefetch=2,
            grid=(count // block,),
            in_specs=[
                pl.BlockSpec((N_DOM, LINES, R), lambda i, *_: (0, 0, 0)),
                pl.BlockSpec((1, block), lambda i, *_: (0, i)),
                pl.BlockSpec((1, block), lambda i, *_: (0, i)),
                pl.BlockSpec((block, R), lambda i, *_: (i, 0)),
            ],
            out_specs=[pl.BlockSpec((HALF, R), whole)] * 2,
            scratch_shapes=[
                pltpu.VMEM((NPART + 16, R), bf16),
                pltpu.VMEM((ROWS, R), f32),
                pltpu.VMEM((ROWS, block), bf16),
                pltpu.VMEM((block, R), bf16),
            ],
        ),
        compiler_params=pltpu.CompilerParams(vmem_limit_bytes=VMEM_LIMIT),
        name="points_pass",
    )(snapshots, core, gathered, observed.reshape(1, count), precision.reshape(1, count), basis)


def tile_at(n):
    return pl.ds(pl.multiple_of(n * 8, 8), 8)


def factor_and_solve(sys_ref, panel_ref, wide_ref, rhs_ref, out_ref):
    tiles = R // 8
    sub = lax.broadcasted_iota(jnp.int32, (8, R), 0)

    def row_of(ref, k, row):
        return jnp.broadcast_to(ref[k, pl.ds(row, 1), :], (8, R))

    def in_one_tile(rows):
        out = rows[0]
        for k in range(1, 8):
            out = jnp.where(sub == k, rows[k], out)
        return out

    def panel(p, carry):
        first = p * 8
        corner = [[row_of(sys_ref, first + k, first + i) if i >= k else None for k in range(8)] for i in range(8)]
        low = [[None] * 8 for _ in range(8)]
        inverse = [None] * 8
        for k in range(8):
            inverse[k] = 1.0 / corner[k][k]
            for i in range(k + 1, 8):
                low[i][k] = corner[i][k] * inverse[k]
            for j in range(k + 1, 8):
                for i in range(j, 8):
                    corner[i][j] = corner[i][j] - corner[i][k] * low[j][k]
        y = [jnp.broadcast_to(rhs_ref[pl.ds(first + k, 1), :], (8, R)) for k in range(8)]
        for k in range(8):
            for m in range(k):
                y[k] = y[k] - low[k][m] * y[m]
        out_ref[tile_at(p), :] = in_one_tile([y[k] * inverse[k] for k in range(8)])

        def below(t, carry):
            at = tile_at(t)
            columns = [sys_ref[first + k, at, :] for k in range(8)]
            rhs = rhs_ref[at, :]
            for k in range(8):
                for m in range(k):
                    columns[k] = columns[k] - columns[m] * low[k][m]
                panel_ref[k, at, :] = columns[k]
                factor = columns[k] * inverse[k]
                sys_ref[first + k, at, :] = factor
                for r in range(8):
                    wide_ref[t * 8 + r, k] = jnp.broadcast_to(factor[r : r + 1], (8, R))
                rhs = rhs - factor * y[k]
            rhs_ref[at, :] = rhs
            return carry

        lax.fori_loop(p, tiles, below, 0)

        def trailing(tj, carry):
            def pair(h, carry):
                at = [tile_at(tj + 2 * h), tile_at(tj + 2 * h + 1)]
                columns = [[panel_ref[k, at[e], :] for k in range(8)] for e in range(2)]
                for j in range(8):
                    row = tj * 8 + j
                    total = [None, None]
                    for k in range(8):
                        factor = wide_ref[row, k]
                        for e in range(2):
                            term = columns[e][k] * factor
                            total[e] = term if k == 0 else total[e] + term
                    for e in range(2):
                        sys_ref[row, at[e], :] = sys_ref[row, at[e], :] - total[e]
                return carry

            return lax.fori_loop(0, (tiles - tj + 1) // 2, pair, carry)

        return lax.fori_loop(p + 1, tiles, trailing, carry)

    lax.fori_loop(0, tiles, panel, 0)

    def back(n, carry):
        p = tiles - 1 - n
        first = p * 8

        def gather(t, sums):
            at = tile_at(t)
            x = out_ref[at, :]
            return tuple(sums[k] + sys_ref[first + k, at, :] * x for k in range(8))

        sums = lax.fori_loop(p + 1, tiles, gather, tuple(jnp.zeros((8, R), f32) for _ in range(8)))
        x = [
            jnp.broadcast_to(out_ref[pl.ds(first + k, 1), :] - jnp.sum(sums[k], axis=0, keepdims=True), (8, R))
            for k in range(8)
        ]
        for k in range(7, 0, -1):
            for m in range(k):
                x[m] = x[m] - row_of(sys_ref, first + m, first + k) * x[k]
        out_ref[tile_at(p), :] = in_one_tile(x)
        return carry

    lax.fori_loop(0, tiles, back, 0)


def in_three(x):
    high = x.astype(bf16).astype(f32)
    middle = (x - high).astype(bf16).astype(f32)
    return high, middle, x - high - middle


def steps_kernel(where_ref, picks_ref, gathered_ref, mine_ref, other_ref, out_ref,
                 sums_ref, sys_ref, panel_ref, wide_ref, rhs_ref, step_ref):
    scale = R / PTS
    core, dom = where_ref[0], where_ref[1]
    for half in range(2):

        @pl.when(core == half)
        def _():
            sums_ref[half * HALF : (half + 1) * HALF, :] = mine_ref[...]
            sums_ref[(1 - half) * HALF : (2 - half) * HALF, :] = other_ref[...]

    lane = lax.broadcasted_iota(jnp.int32, (8, R), 1)
    sub = lax.broadcasted_iota(jnp.int32, (8, R), 0)
    square_r = lax.broadcasted_iota(jnp.int32, (R, R), 0)
    square_q = lax.broadcasted_iota(jnp.int32, (R, R), 1)
    eye = (square_r == square_q).astype(f32)

    everyone = particles(gathered_ref)
    tags = [gathered_ref[d, NP_DEV : NP_DEV + 1, :] for d in range(N_DOM)]
    first_half = lane[0:1] < NP_DEV
    counts = jnp.concatenate(
        [jnp.where(first_half, tags[d], pltpu.roll(tags[d + 1], NP_DEV, 1)) for d in range(0, N_DOM, 2)], axis=1
    )

    owners = pltpu.roll(jnp.concatenate(tags, axis=0), NP_DEV, 1)
    named = jnp.where((owners == dom.astype(f32)) & (lane < NP_DEV), 1.0, 0.0)
    before = jnp.dot(named, (square_r < square_q).astype(f32), precision=highest, preferred_element_type=f32)
    slot = lax.broadcasted_iota(jnp.int32, (16, R), 0).astype(f32)
    own, valid = [], []
    for d in range(N_DOM):
        choose = jnp.where((named[d : d + 1] > 0.5) & (before[d : d + 1] == slot), 1.0, 0.0)
        valid.append(jnp.sum(choose, axis=1, keepdims=True))
        own.append(jnp.dot(choose[:, :NP_DEV], gathered_ref[d, 0:NP_DEV, :], precision=highest,
                           preferred_element_type=f32))
    own, valid = jnp.concatenate(own, axis=0), jnp.concatenate(valid, axis=0)

    mean_hess = sums_ref[NPART : NPART + R, :]
    for s in range(1, SNAP):
        mean_hess = mean_hess + sums_ref[NPART + s * R : NPART + (s + 1) * R, :]
    mean_hess = eye + mean_hess * (scale / SNAP)
    trace = jnp.sum(jnp.sum(mean_hess * eye, axis=1, keepdims=True), axis=0, keepdims=True)
    repulse = 6.0 / trace

    lifted = jnp.dot(everyone, mean_hess, precision=highest, preferred_element_type=f32)
    ones = jnp.ones((8, R), f32)
    norms = lax.dot_general(ones, lifted * everyone, last_pair, precision=highest, preferred_element_type=f32)[0:1]
    own_lift = jnp.dot(own, mean_hess, precision=highest, preferred_element_type=f32)
    own_norm = jnp.sum(own_lift * own, axis=1, keepdims=True)
    cross = lax.dot_general(own_lift, everyone, last_pair, precision=highest, preferred_element_type=f32)
    distance = own_norm + norms - 2.0 * cross
    weights = counts * jnp.exp(-3.0 * distance / trace)
    total = jnp.sum(weights, axis=1, keepdims=True)
    low_weights = weights.astype(bf16)
    carried = (everyone + repulse * lifted).astype(bf16)
    numerator = jnp.dot(low_weights, carried, preferred_element_type=f32)
    grad = jnp.dot(low_weights.astype(f32), sums_ref[0:NPART, :], precision=highest, preferred_element_type=f32)
    drift = -(numerator + scale * grad) / total + repulse * own_lift
    rhs_ref[...] = drift.T

    rows = []
    for s in range(SNAP):
        j = picks_ref[s]
        rows.append(gathered_ref[j // NP_DEV, pl.ds(j % NP_DEV, 1), :])
    rows.append(jnp.zeros((R - SNAP, R), f32))
    picked = jnp.concatenate(rows, axis=0)
    picked_lift = jnp.dot(picked, mean_hess, precision=highest, preferred_element_type=f32)
    picked_norm = lax.dot_general(ones, picked_lift * picked, last_pair, precision=highest,
                                  preferred_element_type=f32)[0:1]
    picked_cross = lax.dot_general(own_lift, picked, last_pair, precision=highest, preferred_element_type=f32)
    apart = 1.0 + (own_norm + picked_norm - 2.0 * picked_cross) / trace
    mixture = jnp.where(square_q < SNAP, 1.0 / (apart * apart), 0.0)
    mixture = mixture / jnp.sum(mixture, axis=1, keepdims=True)
    shares = mixture.T[0:SNAP, :]
    share_sum = jnp.sum(shares, axis=0, keepdims=True)
    high, middle, low = in_three(shares * scale)
    factors = jnp.concatenate([high, middle, low, high, middle, high], axis=0).astype(bf16)

    def assemble(g, carry):
        parts = []
        for k in range(8):
            hess_rows = sums_ref[pl.ds(NPART + g * 8 + k, SNAP, stride=R), :]
            high, middle, low = in_three(hess_rows)
            parts.append(jnp.concatenate([high, high, high, middle, middle, low], axis=0).astype(bf16))
        product = lax.dot_general(jnp.concatenate(parts, axis=1), factors, (((0,), (0,)), ((), ())),
                                  preferred_element_type=f32)
        for k in range(8):
            sys_ref[g * 8 + k, 0:R, :] = product[k * R : (k + 1) * R]
            sys_ref[g * 8 + k, tile_at(g), :] += jnp.where(sub == k, share_sum, 0.0)
        return carry

    lax.fori_loop(0, R // 8, assemble, 0)
    sys_ref[:, R : R + 8, :] = jnp.zeros((R, 8, R), f32)
    panel_ref[:, R : R + 8, :] = jnp.zeros((8, 8, R), f32)
    factor_and_solve(sys_ref, panel_ref, wide_ref, rhs_ref, step_ref)
    out_ref[...] = jnp.where(valid > 0.5, own + step_ref[...].T, 0.0)


def newton_rows(where, snapshots, gathered, mine, other):
    vmem = pl.BlockSpec(memory_space=pltpu.VMEM)
    smem = pl.BlockSpec(memory_space=pltpu.SMEM)
    return pl.pallas_call(
        steps_kernel,
        out_shape=jax.ShapeDtypeStruct((R, R), f32),
        in_specs=[smem, smem, vmem, vmem, vmem],
        out_specs=vmem,
        scratch_shapes=[
            pltpu.VMEM((ROWS, R), f32),
            pltpu.VMEM((R, R + 8, R), f32),
            pltpu.VMEM((8, R + 8, R), f32),
            pltpu.VMEM((R, 8, 8, R), f32),
            pltpu.VMEM((R, R), f32),
            pltpu.VMEM((R, R), f32),
        ],
        compiler_params=pltpu.CompilerParams(vmem_limit_bytes=VMEM_LIMIT),
        name="newton_rows",
    )(where, snapshots, gathered, mine, other)


def sent_to_all(shard, axes):
    copies = jnp.broadcast_to(shard, (lax.axis_size(axes), *shard.shape))
    return lax.all_to_all(copies, axes, split_axis=0, concat_axis=0, tiled=True)


def body(coefficients, copies, owner, snapshots, basis, observed, precision):
    tags = jnp.concatenate([copies, owner[:, 0]]).astype(f32)[None]
    lines = jnp.concatenate([coefficients, tags, jnp.zeros((LINES - NP_DEV - 1, R), f32)], axis=0)
    gathered = sent_to_all(lines, DOM)
    core = lax.axis_index(C)
    swap = [(0, 1), (1, 0)]
    keep, send = points_pass(snapshots, core.reshape(1), gathered, observed, precision, basis)
    part = keep + lax.ppermute(send, C, swap)
    chips = lax.axis_size(CHIPS)
    blocks = lax.all_to_all(part.reshape(chips, HALF // chips, R), CHIPS, 0, 0, tiled=True)
    mine = sent_to_all(jnp.sum(blocks, axis=0), CHIPS).reshape(HALF, R)
    other = lax.ppermute(mine, C, swap)
    where = jnp.stack([core, lax.axis_index(DOM)])
    rows = newton_rows(where, snapshots, gathered, mine, other)
    return rows.reshape(1, N_DOM, 2 * NP_DEV // N_DOM, R)


def solution(mesh):
    finer = Mesh(mesh.devices.reshape(4, 4, 4, 2), FIELD_DOM)
    return jax.shard_map(
        body,
        mesh=finer,
        in_specs=(
            P(DOM, None),
            P(DOM),
            P(DOM, None),
            P(),
            P(FIELD_DOM, None),
            P(FIELD_DOM),
            P(FIELD_DOM),
        ),
        out_specs=P(DOM, None, None, None),
        check_vma=False,
    )
```

```python
import functools

import jax
import jax.numpy as jnp
from jax import lax
from jax.experimental import pallas as pl
from jax.experimental.pallas import tpu as pltpu
from jax.sharding import Mesh
from jax.sharding import PartitionSpec as P

PTS = 4194304
R = 128
NP_DEV = 64
NPART = 512
SNAP = 8
N_DOM = 8
ROWS = NPART + SNAP * R
HALF = ROWS // 2
LINES = 72
X, Z, Y, C = "field_0", "field_1", "dom_0", "dom_1"
DOM = (Y, C)
FIELD = (X, Z)
CHIPS = (X, Z, Y)
FIELD_DOM = (X, Z, Y, C)
f32, bf16 = jnp.float32, jnp.bfloat16
highest = lax.Precision.HIGHEST
last_pair = (((1,), (1,)), ((), ()))
POINTS_VMEM = 55 << 20
STEPS_VMEM = 30 << 20


def lines_kernel(coef_ref, copies_ref, owner_ref, lines_ref):
    row = lax.broadcasted_iota(jnp.int32, (NP_DEV, R), 0)
    lane = lax.broadcasted_iota(jnp.int32, (NP_DEV, R), 1)
    owners = jnp.where(lane == row + NP_DEV, owner_ref[...], 0)
    owners = jnp.sum(owners.astype(f32), axis=0, keepdims=True)
    counts = jnp.concatenate([copies_ref[...].astype(f32), jnp.zeros((1, R - NP_DEV), f32)], axis=1)
    for d in range(N_DOM):
        lines_ref[d, 0:NP_DEV, :] = coef_ref[...]
        lines_ref[d, NP_DEV : NP_DEV + 1, :] = owners + counts
        lines_ref[d, NP_DEV + 1 : LINES, :] = jnp.zeros((LINES - NP_DEV - 1, R), f32)


def packed_lines(coefficients, copies, owner):
    return pl.pallas_call(
        lines_kernel,
        out_shape=jax.ShapeDtypeStruct((N_DOM, LINES, R), f32),
        compiler_params=pltpu.CompilerParams(vmem_limit_bytes=4 << 20),
        name="packed_lines",
    )(coefficients, copies.reshape(1, NP_DEV), owner)


def particles(gathered_ref):
    return jnp.concatenate([gathered_ref[d, 0:NP_DEV, :] for d in range(N_DOM)], axis=0)


def points_kernel(block, chunk, picks_ref, gathered_ref, obs_ref, prec_ref, basis_ref,
                  keep_ref, send_ref, coef_ref, sums_ref, left_ref, right_ref):
    step = pl.program_id(0)

    @pl.when(step == 0)
    def _():
        sums_ref[...] = jnp.zeros_like(sums_ref)
        coef_ref[0:NPART, :] = particles(gathered_ref).astype(bf16)
        rows = []
        for s in range(SNAP):
            j = picks_ref[s]
            rows.append(gathered_ref[j // NP_DEV, pl.ds(j % NP_DEV, 1), :])
        rows.append(jnp.zeros((SNAP, R), f32))
        coef_ref[NPART : NPART + 16, :] = jnp.concatenate(rows, axis=0).astype(bf16)

    for c in range(block // chunk):
        at = pl.ds(c * chunk, chunk)
        rows = basis_ref[at, :]
        columns = rows.T
        prec = prec_ref[:, at]
        right_ref[at, :] = (columns.astype(f32) * prec).astype(bf16).T
        field = lax.dot_general(coef_ref[...], rows, last_pair, preferred_element_type=f32)
        slopes = jnp.tanh(field[: NPART + SNAP] - obs_ref[:, at])
        left_ref[0:NPART, at] = slopes[:NPART].astype(bf16)
        picked = slopes[NPART : NPART + SNAP]
        bend = 1.0 - picked * picked
        for s in range(SNAP):
            top = NPART + s * R
            left_ref[top : top + R, at] = bend[s : s + 1, :].astype(bf16) * columns
    sums_ref[...] += jnp.dot(left_ref[...], right_ref[...], preferred_element_type=f32)

    @pl.when(step == pl.num_programs(0) - 1)
    def _():
        for core in range(2):

            @pl.when(lax.axis_index(C) == core)
            def _():
                keep_ref[...] = sums_ref[core * HALF : (core + 1) * HALF, :]
                send_ref[...] = sums_ref[(1 - core) * HALF : (2 - core) * HALF, :]


def points_pass(snapshots, gathered, observed, precision, basis):
    block, chunk = 4096, 512
    count = basis.shape[0]
    whole = lambda i, *_: (0, 0)
    return pl.pallas_call(
        functools.partial(points_kernel, block, chunk),
        out_shape=[jax.ShapeDtypeStruct((HALF, R), f32)] * 2,
        grid_spec=pltpu.PrefetchScalarGridSpec(
            num_scalar_prefetch=1,
            grid=(count // block,),
            in_specs=[
                pl.BlockSpec((N_DOM, LINES, R), lambda i, *_: (0, 0, 0)),
                pl.BlockSpec((1, block), lambda i, *_: (0, i)),
                pl.BlockSpec((1, block), lambda i, *_: (0, i)),
                pl.BlockSpec((block, R), lambda i, *_: (i, 0)),
            ],
            out_specs=[pl.BlockSpec((HALF, R), whole)] * 2,
            scratch_shapes=[
                pltpu.VMEM((NPART + 16, R), bf16),
                pltpu.VMEM((ROWS, R), f32),
                pltpu.VMEM((ROWS, block), bf16),
                pltpu.VMEM((block, R), bf16),
            ],
        ),
        compiler_params=pltpu.CompilerParams(vmem_limit_bytes=POINTS_VMEM),
        name="points_pass",
    )(snapshots, gathered, observed.reshape(1, count), precision.reshape(1, count), basis)


def tile_at(n):
    return pl.ds(pl.multiple_of(n * 8, 8), 8)


def factor_and_solve(sys_ref, panel_ref, wide_ref, rhs_ref, out_ref):
    tiles = R // 8
    sub = lax.broadcasted_iota(jnp.int32, (8, R), 0)

    def row_of(ref, k, row):
        return jnp.broadcast_to(ref[k, pl.ds(row, 1), :], (8, R))

    def in_one_tile(rows):
        out = rows[0]
        for k in range(1, 8):
            out = jnp.where(sub == k, rows[k], out)
        return out

    def panel(p, carry):
        first = p * 8
        corner = [[row_of(sys_ref, first + k, first + i) if i >= k else None for k in range(8)] for i in range(8)]
        low = [[None] * 8 for _ in range(8)]
        inverse = [None] * 8
        for k in range(8):
            inverse[k] = 1.0 / corner[k][k]
            for i in range(k + 1, 8):
                low[i][k] = corner[i][k] * inverse[k]
            for j in range(k + 1, 8):
                for i in range(j, 8):
                    corner[i][j] = corner[i][j] - corner[i][k] * low[j][k]
        y = [jnp.broadcast_to(rhs_ref[pl.ds(first + k, 1), :], (8, R)) for k in range(8)]
        for k in range(8):
            for m in range(k):
                y[k] = y[k] - low[k][m] * y[m]
        out_ref[tile_at(p), :] = in_one_tile([y[k] * inverse[k] for k in range(8)])

        def below(t, carry):
            at = tile_at(t)
            columns = [sys_ref[first + k, at, :] for k in range(8)]
            rhs = rhs_ref[at, :]
            for k in range(8):
                for m in range(k):
                    columns[k] = columns[k] - columns[m] * low[k][m]
                panel_ref[k, at, :] = columns[k]
                factor = columns[k] * inverse[k]
                sys_ref[first + k, at, :] = factor
                for r in range(8):
                    wide_ref[t * 8 + r, k] = jnp.broadcast_to(factor[r : r + 1], (8, R))
                rhs = rhs - factor * y[k]
            rhs_ref[at, :] = rhs
            return carry

        lax.fori_loop(p, tiles, below, 0)

        def trailing(tj, carry):
            def group(size, start, h, carry):
                at = [tile_at(start + size * h + e) for e in range(size)]
                columns = [[panel_ref[k, at[e], :] for k in range(8)] for e in range(size)]
                for j in range(8):
                    row = tj * 8 + j
                    total = [None] * size
                    for k in range(8):
                        factor = wide_ref[row, k]
                        for e in range(size):
                            term = columns[e][k] * factor
                            total[e] = term if k == 0 else total[e] + term
                    for e in range(size):
                        sys_ref[row, at[e], :] = sys_ref[row, at[e], :] - total[e]
                return carry

            rest = (tiles - tj) % 3
            lax.fori_loop(0, rest, functools.partial(group, 1, tj), carry)
            return lax.fori_loop(0, (tiles - tj) // 3, functools.partial(group, 3, tj + rest), carry)

        return lax.fori_loop(p + 1, tiles, trailing, carry)

    lax.fori_loop(0, tiles, panel, 0)

    def back(n, carry):
        p = tiles - 1 - n
        first = p * 8

        def gather(t, sums):
            at = tile_at(t)
            x = out_ref[at, :]
            return tuple(sums[k] + sys_ref[first + k, at, :] * x for k in range(8))

        sums = lax.fori_loop(p + 1, tiles, gather, tuple(jnp.zeros((8, R), f32) for _ in range(8)))
        x = [
            jnp.broadcast_to(out_ref[pl.ds(first + k, 1), :] - jnp.sum(sums[k], axis=0, keepdims=True), (8, R))
            for k in range(8)
        ]
        for k in range(7, 0, -1):
            for m in range(k):
                x[m] = x[m] - row_of(sys_ref, first + m, first + k) * x[k]
        out_ref[tile_at(p), :] = in_one_tile(x)
        return carry

    lax.fori_loop(0, tiles, back, 0)


def in_three(x):
    high = x.astype(bf16).astype(f32)
    middle = (x - high).astype(bf16).astype(f32)
    return high, middle, x - high - middle


def steps_kernel(picks_ref, gathered_ref, mine_ref, other_ref, out_ref,
                 sums_ref, sys_ref, panel_ref, wide_ref, rhs_ref, step_ref):
    scale = R / PTS
    core, dom = lax.axis_index(C), lax.axis_index(DOM)
    for half in range(2):

        @pl.when(core == half)
        def _():
            sums_ref[half * HALF : (half + 1) * HALF, :] = mine_ref[...]
            sums_ref[(1 - half) * HALF : (2 - half) * HALF, :] = other_ref[...]

    lane = lax.broadcasted_iota(jnp.int32, (8, R), 1)
    sub = lax.broadcasted_iota(jnp.int32, (8, R), 0)
    square_r = lax.broadcasted_iota(jnp.int32, (R, R), 0)
    square_q = lax.broadcasted_iota(jnp.int32, (R, R), 1)
    eye = (square_r == square_q).astype(f32)

    everyone = particles(gathered_ref)
    tags = [gathered_ref[d, NP_DEV : NP_DEV + 1, :] for d in range(N_DOM)]
    first_half = lane[0:1] < NP_DEV
    counts = jnp.concatenate(
        [jnp.where(first_half, tags[d], pltpu.roll(tags[d + 1], NP_DEV, 1)) for d in range(0, N_DOM, 2)], axis=1
    )

    owners = pltpu.roll(jnp.concatenate(tags, axis=0), NP_DEV, 1)
    named = jnp.where((owners == dom.astype(f32)) & (lane < NP_DEV), 1.0, 0.0)
    before = jnp.dot(named, (square_r < square_q).astype(f32), precision=highest, preferred_element_type=f32)
    slot = lax.broadcasted_iota(jnp.int32, (16, R), 0).astype(f32)
    own, valid = [], []
    for d in range(N_DOM):
        choose = jnp.where((named[d : d + 1] > 0.5) & (before[d : d + 1] == slot), 1.0, 0.0)
        valid.append(jnp.sum(choose, axis=1, keepdims=True))
        own.append(jnp.dot(choose[:, :NP_DEV], gathered_ref[d, 0:NP_DEV, :], precision=highest,
                           preferred_element_type=f32))
    own, valid = jnp.concatenate(own, axis=0), jnp.concatenate(valid, axis=0)

    mean_hess = sums_ref[NPART : NPART + R, :]
    for s in range(1, SNAP):
        mean_hess = mean_hess + sums_ref[NPART + s * R : NPART + (s + 1) * R, :]
    mean_hess = eye + mean_hess * (scale / SNAP)
    trace = jnp.sum(jnp.sum(mean_hess * eye, axis=1, keepdims=True), axis=0, keepdims=True)
    repulse = 6.0 / trace

    lifted = jnp.dot(everyone, mean_hess, precision=highest, preferred_element_type=f32)
    ones = jnp.ones((8, R), f32)
    norms = lax.dot_general(ones, lifted * everyone, last_pair, precision=highest, preferred_element_type=f32)[0:1]
    own_lift = jnp.dot(own, mean_hess, precision=highest, preferred_element_type=f32)
    own_norm = jnp.sum(own_lift * own, axis=1, keepdims=True)
    cross = lax.dot_general(own_lift, everyone, last_pair, precision=highest, preferred_element_type=f32)
    distance = own_norm + norms - 2.0 * cross
    weights = counts * jnp.exp(-3.0 * distance / trace)
    total = jnp.sum(weights, axis=1, keepdims=True)
    low_weights = weights.astype(bf16)
    carried = (everyone + repulse * lifted).astype(bf16)
    numerator = jnp.dot(low_weights, carried, preferred_element_type=f32)
    grad = jnp.dot(low_weights.astype(f32), sums_ref[0:NPART, :], precision=highest, preferred_element_type=f32)
    drift = -(numerator + scale * grad) / total + repulse * own_lift
    rhs_ref[...] = drift.T

    rows = []
    for s in range(SNAP):
        j = picks_ref[s]
        rows.append(gathered_ref[j // NP_DEV, pl.ds(j % NP_DEV, 1), :])
    rows.append(jnp.zeros((R - SNAP, R), f32))
    picked = jnp.concatenate(rows, axis=0)
    picked_lift = jnp.dot(picked, mean_hess, precision=highest, preferred_element_type=f32)
    picked_norm = lax.dot_general(ones, picked_lift * picked, last_pair, precision=highest,
                                  preferred_element_type=f32)[0:1]
    picked_cross = lax.dot_general(own_lift, picked, last_pair, precision=highest, preferred_element_type=f32)
    apart = 1.0 + (own_norm + picked_norm - 2.0 * picked_cross) / trace
    mixture = jnp.where(square_q < SNAP, 1.0 / (apart * apart), 0.0)
    mixture = mixture / jnp.sum(mixture, axis=1, keepdims=True)
    shares = mixture.T[0:SNAP, :]
    share_sum = jnp.sum(shares, axis=0, keepdims=True)
    high, middle, low = in_three(shares * scale)
    factors = jnp.concatenate([high, middle, low, high, middle, high], axis=0).astype(bf16)

    def assemble(g, carry):
        parts = []
        for k in range(8):
            hess_rows = sums_ref[pl.ds(NPART + g * 8 + k, SNAP, stride=R), :]
            high, middle, low = in_three(hess_rows)
            parts.append(jnp.concatenate([high, high, high, middle, middle, low], axis=0).astype(bf16))
        product = lax.dot_general(jnp.concatenate(parts, axis=1), factors, (((0,), (0,)), ((), ())),
                                  preferred_element_type=f32)
        for k in range(8):
            sys_ref[g * 8 + k] = product[k * R : (k + 1) * R]
            sys_ref[g * 8 + k, tile_at(g), :] += jnp.where(sub == k, share_sum, 0.0)
        return carry

    lax.fori_loop(0, R // 8, assemble, 0, unroll=4)
    factor_and_solve(sys_ref, panel_ref, wide_ref, rhs_ref, step_ref)
    out_ref[...] = jnp.where(valid > 0.5, own + step_ref[...].T, 0.0)


def newton_rows(snapshots, gathered, mine, other):
    vmem = pl.BlockSpec(memory_space=pltpu.VMEM)
    smem = pl.BlockSpec(memory_space=pltpu.SMEM)
    return pl.pallas_call(
        steps_kernel,
        out_shape=jax.ShapeDtypeStruct((R, R), f32),
        in_specs=[smem, vmem, vmem, vmem],
        out_specs=vmem,
        scratch_shapes=[
            pltpu.VMEM((ROWS, R), f32),
            pltpu.VMEM((R, R, R), f32),
            pltpu.VMEM((8, R, R), f32),
            pltpu.VMEM((R, 8, 8, R), f32),
            pltpu.VMEM((R, R), f32),
            pltpu.VMEM((R, R), f32),
        ],
        compiler_params=pltpu.CompilerParams(vmem_limit_bytes=STEPS_VMEM),
        name="newton_rows",
    )(snapshots, gathered, mine, other)


def sent_to_all(shard, axes):
    copies = jnp.broadcast_to(shard, (lax.axis_size(axes), *shard.shape))
    return lax.all_to_all(copies, axes, split_axis=0, concat_axis=0, tiled=True)


def body(coefficients, copies, owner, snapshots, basis, observed, precision):
    lines = packed_lines(coefficients, copies, owner)
    gathered = lax.all_to_all(lines, DOM, split_axis=0, concat_axis=0, tiled=True)
    swap = [(0, 1), (1, 0)]
    keep, send = points_pass(snapshots, gathered, observed, precision, basis)
    part = keep + lax.ppermute(send, C, swap)
    chips = lax.axis_size(CHIPS)
    blocks = lax.all_to_all(part.reshape(chips, HALF // chips, R), CHIPS, 0, 0, tiled=True)
    mine = sent_to_all(jnp.sum(blocks, axis=0), CHIPS).reshape(HALF, R)
    other = lax.ppermute(mine, C, swap)
    rows = newton_rows(snapshots, gathered, mine, other)
    return rows.reshape(1, N_DOM, 2 * NP_DEV // N_DOM, R)


def solution(mesh):
    finer = Mesh(mesh.devices.reshape(4, 4, 4, 2), FIELD_DOM)
    return jax.shard_map(
        body,
        mesh=finer,
        in_specs=(
            P(DOM, None),
            P(DOM),
            P(DOM, None),
            P(),
            P(FIELD_DOM, None),
            P(FIELD_DOM),
            P(FIELD_DOM),
        ),
        out_specs=P(DOM, None, None, None),
        check_vma=False,
    )
```

```python
import functools

import jax
import jax.numpy as jnp
from jax import lax
from jax.experimental import pallas as pl
from jax.experimental.pallas import tpu as pltpu
from jax.sharding import Mesh
from jax.sharding import PartitionSpec as P

PTS = 4194304
R = 128
NP_DEV = 64
NPART = 512
SNAP = 8
N_DOM = 8
ROWS = NPART + SNAP * R
HALF = ROWS // 2
LINES = 72
X, Z, Y, C = "field_0", "field_1", "dom_0", "dom_1"
DOM = (Y, C)
FIELD = (X, Z)
CHIPS = (X, Z, Y)
FIELD_DOM = (X, Z, Y, C)
f32, bf16 = jnp.float32, jnp.bfloat16
highest = lax.Precision.HIGHEST
last_pair = (((1,), (1,)), ((), ()))
POINTS_VMEM = 51 << 20
STEPS_VMEM = 30 << 20


def lines_kernel(coef_ref, copies_ref, owner_ref, lines_ref):
    lines_ref[0:NP_DEV, :] = coef_ref[...]
    tags = jnp.concatenate([copies_ref[...], owner_ref[...]], axis=1).astype(f32)
    lines_ref[NP_DEV:LINES, :] = jnp.broadcast_to(tags, (LINES - NP_DEV, R))


def packed_lines(coefficients, copies, owner):
    return pl.pallas_call(
        lines_kernel,
        out_shape=jax.ShapeDtypeStruct((LINES, R), f32),
        compiler_params=pltpu.CompilerParams(vmem_limit_bytes=60 << 20),
        name="packed_lines",
    )(coefficients, copies.reshape(1, NP_DEV), owner.reshape(1, NP_DEV))


def particles(gathered_ref):
    return jnp.concatenate([gathered_ref[d, 0:NP_DEV, :] for d in range(N_DOM)], axis=0)


def points_kernel(block, chunk, picks_ref, near_ref, one_ref, two_ref, three_ref, obs_ref, prec_ref, basis_ref,
                  gathered_ref, keep_ref, send_ref, coef_ref, sums_ref, left_ref, right_ref):
    step = pl.program_id(0)

    @pl.when(step == 0)
    def _():
        sums_ref[...] = jnp.zeros_like(sums_ref)
        y, core = lax.axis_index(Y), lax.axis_index(C)
        for shift, pair_ref in enumerate((near_ref, one_ref, two_ref, three_ref)):
            for j in range(2):
                source = (y + 4 - shift) % 4 * 2 + (core + j) % 2
                gathered_ref[source] = pair_ref[j * LINES : (j + 1) * LINES, :]
        coef_ref[0:NPART, :] = particles(gathered_ref).astype(bf16)
        rows = []
        for s in range(SNAP):
            j = picks_ref[s]
            rows.append(gathered_ref[j // NP_DEV, pl.ds(j % NP_DEV, 1), :])
        rows.append(jnp.zeros((SNAP, R), f32))
        coef_ref[NPART : NPART + 16, :] = jnp.concatenate(rows, axis=0).astype(bf16)

    for c in range(block // chunk):
        at = pl.ds(c * chunk, chunk)
        rows = basis_ref[at, :]
        columns = rows.T
        prec = prec_ref[:, at]
        right_ref[at, :] = (columns.astype(f32) * prec).astype(bf16).T
        field = lax.dot_general(coef_ref[...], rows, last_pair, preferred_element_type=f32)
        slopes = jnp.tanh(field[: NPART + SNAP] - obs_ref[:, at])
        left_ref[0:NPART, at] = slopes[:NPART].astype(bf16)
        picked = slopes[NPART : NPART + SNAP]
        bend = 1.0 - picked * picked
        for s in range(SNAP):
            top = NPART + s * R
            left_ref[top : top + R, at] = bend[s : s + 1, :].astype(bf16) * columns
    sums_ref[...] += jnp.dot(left_ref[...], right_ref[...], preferred_element_type=f32)

    @pl.when(step == pl.num_programs(0) - 1)
    def _():
        for core in range(2):

            @pl.when(lax.axis_index(C) == core)
            def _():
                keep_ref[...] = sums_ref[core * HALF : (core + 1) * HALF, :]
                send_ref[...] = sums_ref[(1 - core) * HALF : (2 - core) * HALF, :]


def in_hbm(x):
    return pltpu.with_memory_space_constraint(x, pltpu.HBM)


def points_pass(snapshots, pairs, observed, precision, basis):
    block, chunk = 4096, 512
    count = basis.shape[0]
    whole = lambda i, *_: (0, 0)
    return pl.pallas_call(
        functools.partial(points_kernel, block, chunk),
        out_shape=[jax.ShapeDtypeStruct((N_DOM, LINES, R), f32)] + [jax.ShapeDtypeStruct((HALF, R), f32)] * 2,
        grid_spec=pltpu.PrefetchScalarGridSpec(
            num_scalar_prefetch=1,
            grid=(count // block,),
            in_specs=[
                *[pl.BlockSpec((2 * LINES, R), whole)] * 4,
                pl.BlockSpec((1, block), lambda i, *_: (0, i)),
                pl.BlockSpec((1, block), lambda i, *_: (0, i)),
                pl.BlockSpec((block, R), lambda i, *_: (i, 0)),
            ],
            out_specs=[pl.BlockSpec((N_DOM, LINES, R), lambda i, *_: (0, 0, 0))] + [pl.BlockSpec((HALF, R), whole)] * 2,
            scratch_shapes=[
                pltpu.VMEM((NPART + 16, R), bf16),
                pltpu.VMEM((ROWS, R), f32),
                pltpu.VMEM((ROWS, block), bf16),
                pltpu.VMEM((block, R), bf16),
            ],
        ),
        compiler_params=pltpu.CompilerParams(vmem_limit_bytes=POINTS_VMEM),
        name="points_pass",
    )(in_hbm(snapshots), *pairs, *[in_hbm(a.reshape(1, count)) for a in (observed, precision)], basis)


def tile_at(n):
    return pl.ds(pl.multiple_of(n * 8, 8), 8)


def factor_and_solve(sys_ref, panel_ref, wide_ref, rhs_ref, out_ref):
    tiles = R // 8
    sub = lax.broadcasted_iota(jnp.int32, (8, R), 0)

    def row_of(ref, k, row):
        return jnp.broadcast_to(ref[k, pl.ds(row, 1), :], (8, R))

    def in_one_tile(rows):
        out = rows[0]
        for k in range(1, 8):
            out = jnp.where(sub == k, rows[k], out)
        return out

    def panel(p, carry):
        first = p * 8
        corner = [[row_of(sys_ref, first + k, first + i) if i >= k else None for k in range(8)] for i in range(8)]
        low = [[None] * 8 for _ in range(8)]
        inverse = [None] * 8
        for k in range(8):
            inverse[k] = 1.0 / corner[k][k]
            for i in range(k + 1, 8):
                low[i][k] = corner[i][k] * inverse[k]
            for j in range(k + 1, 8):
                for i in range(j, 8):
                    corner[i][j] = corner[i][j] - corner[i][k] * low[j][k]
        y = [jnp.broadcast_to(rhs_ref[pl.ds(first + k, 1), :], (8, R)) for k in range(8)]
        for k in range(8):
            for m in range(k):
                y[k] = y[k] - low[k][m] * y[m]
        out_ref[tile_at(p), :] = in_one_tile([y[k] * inverse[k] for k in range(8)])

        def below(t, carry):
            at = tile_at(t)
            columns = [sys_ref[first + k, at, :] for k in range(8)]
            rhs = rhs_ref[at, :]
            for k in range(8):
                for m in range(k):
                    columns[k] = columns[k] - columns[m] * low[k][m]
                panel_ref[k, at, :] = columns[k]
                factor = columns[k] * inverse[k]
                sys_ref[first + k, at, :] = factor
                for r in range(8):
                    wide_ref[t * 8 + r, k] = jnp.broadcast_to(factor[r : r + 1], (8, R))
                rhs = rhs - factor * y[k]
            rhs_ref[at, :] = rhs
            return carry

        lax.fori_loop(p, tiles, below, 0)

        def trailing(tj, carry):
            def group(size, start, h, carry):
                at = [tile_at(start + size * h + e) for e in range(size)]
                columns = [[panel_ref[k, at[e], :] for k in range(8)] for e in range(size)]
                for j in range(8):
                    row = tj * 8 + j
                    total = [None] * size
                    for k in range(8):
                        factor = wide_ref[row, k]
                        for e in range(size):
                            term = columns[e][k] * factor
                            total[e] = term if k == 0 else total[e] + term
                    for e in range(size):
                        sys_ref[row, at[e], :] = sys_ref[row, at[e], :] - total[e]
                return carry

            rest = (tiles - tj) % 3
            lax.fori_loop(0, rest, functools.partial(group, 1, tj), carry)
            return lax.fori_loop(0, (tiles - tj) // 3, functools.partial(group, 3, tj + rest), carry)

        return lax.fori_loop(p + 1, tiles, trailing, carry)

    lax.fori_loop(0, tiles, panel, 0)

    def back(n, carry):
        p = tiles - 1 - n
        first = p * 8

        def gather(t, sums):
            at = tile_at(t)
            x = out_ref[at, :]
            return tuple(sums[k] + sys_ref[first + k, at, :] * x for k in range(8))

        sums = lax.fori_loop(p + 1, tiles, gather, tuple(jnp.zeros((8, R), f32) for _ in range(8)))
        x = [
            jnp.broadcast_to(out_ref[pl.ds(first + k, 1), :] - jnp.sum(sums[k], axis=0, keepdims=True), (8, R))
            for k in range(8)
        ]
        for k in range(7, 0, -1):
            for m in range(k):
                x[m] = x[m] - row_of(sys_ref, first + m, first + k) * x[k]
        out_ref[tile_at(p), :] = in_one_tile(x)
        return carry

    lax.fori_loop(0, tiles, back, 0)


def in_three(x):
    high = x.astype(bf16).astype(f32)
    middle = (x - high).astype(bf16).astype(f32)
    return high, middle, x - high - middle


def steps_kernel(picks_ref, gathered_ref, mine_ref, other_ref, out_ref,
                 sums_ref, sys_ref, panel_ref, wide_ref, rhs_ref, step_ref):
    scale = R / PTS
    core, dom = lax.axis_index(C), lax.axis_index(DOM)
    for half in range(2):

        @pl.when(core == half)
        def _():
            sums_ref[half * HALF : (half + 1) * HALF, :] = mine_ref[...]
            sums_ref[(1 - half) * HALF : (2 - half) * HALF, :] = other_ref[...]

    lane = lax.broadcasted_iota(jnp.int32, (8, R), 1)
    sub = lax.broadcasted_iota(jnp.int32, (8, R), 0)
    square_r = lax.broadcasted_iota(jnp.int32, (R, R), 0)
    square_q = lax.broadcasted_iota(jnp.int32, (R, R), 1)
    eye = (square_r == square_q).astype(f32)

    everyone = particles(gathered_ref)
    tags = [gathered_ref[d, NP_DEV : NP_DEV + 1, :] for d in range(N_DOM)]
    first_half = lane[0:1] < NP_DEV
    counts = jnp.concatenate(
        [jnp.where(first_half, tags[d], pltpu.roll(tags[d + 1], NP_DEV, 1)) for d in range(0, N_DOM, 2)], axis=1
    )

    owners = pltpu.roll(jnp.concatenate(tags, axis=0), NP_DEV, 1)
    named = jnp.where((owners == dom.astype(f32)) & (lane < NP_DEV), 1.0, 0.0)
    before = jnp.dot(named, (square_r < square_q).astype(f32), precision=highest, preferred_element_type=f32)
    slot = lax.broadcasted_iota(jnp.int32, (16, R), 0).astype(f32)
    own, valid = [], []
    for d in range(N_DOM):
        choose = jnp.where((named[d : d + 1] > 0.5) & (before[d : d + 1] == slot), 1.0, 0.0)
        valid.append(jnp.sum(choose, axis=1, keepdims=True))
        own.append(jnp.dot(choose[:, :NP_DEV], gathered_ref[d, 0:NP_DEV, :], precision=highest,
                           preferred_element_type=f32))
    own, valid = jnp.concatenate(own, axis=0), jnp.concatenate(valid, axis=0)

    mean_hess = sums_ref[NPART : NPART + R, :]
    for s in range(1, SNAP):
        mean_hess = mean_hess + sums_ref[NPART + s * R : NPART + (s + 1) * R, :]
    mean_hess = eye + mean_hess * (scale / SNAP)
    trace = jnp.sum(jnp.sum(mean_hess * eye, axis=1, keepdims=True), axis=0, keepdims=True)
    repulse = 6.0 / trace

    lifted = jnp.dot(everyone, mean_hess, precision=highest, preferred_element_type=f32)
    ones = jnp.ones((8, R), f32)
    norms = lax.dot_general(ones, lifted * everyone, last_pair, precision=highest, preferred_element_type=f32)[0:1]
    own_lift = jnp.dot(own, mean_hess, precision=highest, preferred_element_type=f32)
    own_norm = jnp.sum(own_lift * own, axis=1, keepdims=True)
    cross = lax.dot_general(own_lift, everyone, last_pair, precision=highest, preferred_element_type=f32)
    distance = own_norm + norms - 2.0 * cross
    weights = counts * jnp.exp(-3.0 * distance / trace)
    total = jnp.sum(weights, axis=1, keepdims=True)
    low_weights = weights.astype(bf16)
    carried = (everyone + repulse * lifted).astype(bf16)
    numerator = jnp.dot(low_weights, carried, preferred_element_type=f32)
    grad = jnp.dot(low_weights.astype(f32), sums_ref[0:NPART, :], precision=highest, preferred_element_type=f32)
    drift = -(numerator + scale * grad) / total + repulse * own_lift
    rhs_ref[...] = drift.T

    rows = []
    for s in range(SNAP):
        j = picks_ref[s]
        rows.append(gathered_ref[j // NP_DEV, pl.ds(j % NP_DEV, 1), :])
    rows.append(jnp.zeros((R - SNAP, R), f32))
    picked = jnp.concatenate(rows, axis=0)
    picked_lift = jnp.dot(picked, mean_hess, precision=highest, preferred_element_type=f32)
    picked_norm = lax.dot_general(ones, picked_lift * picked, last_pair, precision=highest,
                                  preferred_element_type=f32)[0:1]
    picked_cross = lax.dot_general(own_lift, picked, last_pair, precision=highest, preferred_element_type=f32)
    apart = 1.0 + (own_norm + picked_norm - 2.0 * picked_cross) / trace
    mixture = jnp.where(square_q < SNAP, 1.0 / (apart * apart), 0.0)
    mixture = mixture / jnp.sum(mixture, axis=1, keepdims=True)
    shares = mixture.T[0:SNAP, :]
    share_sum = jnp.sum(shares, axis=0, keepdims=True)
    high, middle, low = in_three(shares * scale)
    factors = jnp.concatenate([high, middle, low, high, middle, high], axis=0).astype(bf16)

    def assemble(g, carry):
        parts = []
        for k in range(8):
            hess_rows = sums_ref[pl.ds(NPART + g * 8 + k, SNAP, stride=R), :]
            high, middle, low = in_three(hess_rows)
            parts.append(jnp.concatenate([high, high, high, middle, middle, low], axis=0).astype(bf16))
        product = lax.dot_general(jnp.concatenate(parts, axis=1), factors, (((0,), (0,)), ((), ())),
                                  preferred_element_type=f32)
        for k in range(8):
            sys_ref[g * 8 + k] = product[k * R : (k + 1) * R]
            sys_ref[g * 8 + k, tile_at(g), :] += jnp.where(sub == k, share_sum, 0.0)
        return carry

    lax.fori_loop(0, R // 8, assemble, 0, unroll=4)
    factor_and_solve(sys_ref, panel_ref, wide_ref, rhs_ref, step_ref)
    out_ref[...] = jnp.where(valid > 0.5, own + step_ref[...].T, 0.0)


def newton_rows(snapshots, gathered, mine, other):
    vmem = pl.BlockSpec(memory_space=pltpu.VMEM)
    smem = pl.BlockSpec(memory_space=pltpu.SMEM)
    return pl.pallas_call(
        steps_kernel,
        out_shape=jax.ShapeDtypeStruct((R, R), f32),
        in_specs=[smem, vmem, vmem, vmem],
        out_specs=vmem,
        scratch_shapes=[
            pltpu.VMEM((ROWS, R), f32),
            pltpu.VMEM((R, R, R), f32),
            pltpu.VMEM((8, R, R), f32),
            pltpu.VMEM((R, 8, 8, R), f32),
            pltpu.VMEM((R, R), f32),
            pltpu.VMEM((R, R), f32),
        ],
        compiler_params=pltpu.CompilerParams(vmem_limit_bytes=STEPS_VMEM),
        name="newton_rows",
    )(snapshots, gathered, mine, other)


def sent_to_all(shard, axes):
    copies = jnp.broadcast_to(shard, (lax.axis_size(axes), *shard.shape))
    return lax.all_to_all(copies, axes, split_axis=0, concat_axis=0, tiled=True)


def body(coefficients, copies, owner, snapshots, basis, observed, precision):
    swap = [(0, 1), (1, 0)]
    lines = packed_lines(coefficients, copies, owner)
    pair = jnp.concatenate([lines, lax.ppermute(lines, C, swap)], axis=0)
    pairs = [pair] + [lax.ppermute(pair, Y, [(y, (y + shift) % 4) for y in range(4)]) for shift in (1, 2, 3)]
    gathered, keep, send = points_pass(snapshots, pairs, observed, precision, basis)
    part = keep + lax.ppermute(send, C, swap)
    chips = lax.axis_size(CHIPS)
    blocks = lax.all_to_all(part.reshape(chips, HALF // chips, R), CHIPS, 0, 0, tiled=True)
    mine = sent_to_all(jnp.sum(blocks, axis=0), CHIPS).reshape(HALF, R)
    other = lax.ppermute(mine, C, swap)
    rows = newton_rows(snapshots, gathered, mine, other)
    return rows.reshape(1, N_DOM, 2 * NP_DEV // N_DOM, R)


def solution(mesh):
    finer = Mesh(mesh.devices.reshape(4, 4, 4, 2), FIELD_DOM)
    return jax.shard_map(
        body,
        mesh=finer,
        in_specs=(
            P(DOM, None),
            P(DOM),
            P(DOM, None),
            P(),
            P(FIELD_DOM, None),
            P(FIELD_DOM),
            P(FIELD_DOM),
        ),
        out_specs=P(DOM, None, None, None),
        check_vma=False,
    )
```

```python
import functools

import jax
import jax.numpy as jnp
from jax import lax
from jax.experimental import pallas as pl
from jax.experimental.pallas import tpu as pltpu
from jax.sharding import Mesh
from jax.sharding import PartitionSpec as P

PTS = 4194304
R = 128
NP_DEV = 64
NPART = 512
SNAP = 8
N_DOM = 8
ROWS = NPART + SNAP * R
HALF = ROWS // 2
LINES = 72
X, Z, Y, C = "field_0", "field_1", "dom_0", "dom_1"
DOM = (Y, C)
FIELD = (X, Z)
CHIPS = (X, Z, Y)
FIELD_DOM = (X, Z, Y, C)
f32, bf16 = jnp.float32, jnp.bfloat16
highest = lax.Precision.HIGHEST
last_pair = (((1,), (1,)), ((), ()))
POINTS_VMEM = 51 << 20
STEPS_VMEM = 30 << 20


def lines_kernel(coef_ref, copies_ref, owner_ref, lines_ref):
    lines_ref[0:NP_DEV, :] = coef_ref[...]
    tags = jnp.concatenate([copies_ref[...], owner_ref[...]], axis=1).astype(f32)
    lines_ref[NP_DEV:LINES, :] = jnp.broadcast_to(tags, (LINES - NP_DEV, R))


def packed_lines(coefficients, copies, owner):
    return pl.pallas_call(
        lines_kernel,
        out_shape=jax.ShapeDtypeStruct((LINES, R), f32),
        compiler_params=pltpu.CompilerParams(vmem_limit_bytes=60 << 20),
        name="packed_lines",
    )(coefficients, copies.reshape(1, NP_DEV), owner.reshape(1, NP_DEV))


def particles(gathered_ref):
    return jnp.concatenate([gathered_ref[d, 0:NP_DEV, :] for d in range(N_DOM)], axis=0)


def points_kernel(block, chunk, picks_ref, near_ref, one_ref, two_ref, three_ref, obs_ref, prec_ref, basis_ref,
                  gathered_ref, keep_ref, send_ref, coef_ref, sums_ref, left_ref, right_ref):
    step = pl.program_id(0)

    @pl.when(step == 0)
    def _():
        sums_ref[...] = jnp.zeros_like(sums_ref)
        y = lax.axis_index(Y)
        for shift, pair_ref in enumerate((near_ref, one_ref, two_ref, three_ref)):
            for j in range(2):
                source = (y + 4 - shift) % 4 * 2 + j
                gathered_ref[source] = pair_ref[j * LINES : (j + 1) * LINES, :]
        coef_ref[0:NPART, :] = particles(gathered_ref).astype(bf16)
        rows = []
        for s in range(SNAP):
            j = picks_ref[s]
            rows.append(gathered_ref[j // NP_DEV, pl.ds(j % NP_DEV, 1), :])
        rows.append(jnp.zeros((SNAP, R), f32))
        coef_ref[NPART : NPART + 16, :] = jnp.concatenate(rows, axis=0).astype(bf16)

    for c in range(block // chunk):
        at = pl.ds(c * chunk, chunk)
        rows = basis_ref[at, :]
        columns = rows.T
        prec = prec_ref[:, at]
        right_ref[at, :] = (columns.astype(f32) * prec).astype(bf16).T
        field = lax.dot_general(coef_ref[...], rows, last_pair, preferred_element_type=f32)
        slopes = jnp.tanh(field[: NPART + SNAP] - obs_ref[:, at])
        left_ref[0:NPART, at] = slopes[:NPART].astype(bf16)
        picked = slopes[NPART : NPART + SNAP]
        bend = 1.0 - picked * picked
        for s in range(SNAP):
            top = NPART + s * R
            left_ref[top : top + R, at] = bend[s : s + 1, :].astype(bf16) * columns
    sums_ref[...] += jnp.dot(left_ref[...], right_ref[...], preferred_element_type=f32)

    @pl.when(step == pl.num_programs(0) - 1)
    def _():
        for core in range(2):

            @pl.when(lax.axis_index(C) == core)
            def _():
                keep_ref[...] = sums_ref[core * HALF : (core + 1) * HALF, :]
                send_ref[...] = sums_ref[(1 - core) * HALF : (2 - core) * HALF, :]


def in_hbm(x):
    return pltpu.with_memory_space_constraint(x, pltpu.HBM)


def points_pass(snapshots, pairs, observed, precision, basis):
    block, chunk = 4096, 512
    count = basis.shape[0]
    whole = lambda i, *_: (0, 0)
    return pl.pallas_call(
        functools.partial(points_kernel, block, chunk),
        out_shape=[jax.ShapeDtypeStruct((N_DOM, LINES, R), f32)] + [jax.ShapeDtypeStruct((HALF, R), f32)] * 2,
        grid_spec=pltpu.PrefetchScalarGridSpec(
            num_scalar_prefetch=1,
            grid=(count // block,),
            in_specs=[
                *[pl.BlockSpec((2 * LINES, R), whole)] * 4,
                pl.BlockSpec((1, block), lambda i, *_: (0, i)),
                pl.BlockSpec((1, block), lambda i, *_: (0, i)),
                pl.BlockSpec((block, R), lambda i, *_: (i, 0)),
            ],
            out_specs=[pl.BlockSpec((N_DOM, LINES, R), lambda i, *_: (0, 0, 0))] + [pl.BlockSpec((HALF, R), whole)] * 2,
            scratch_shapes=[
                pltpu.VMEM((NPART + 16, R), bf16),
                pltpu.VMEM((ROWS, R), f32),
                pltpu.VMEM((ROWS, block), bf16),
                pltpu.VMEM((block, R), bf16),
            ],
        ),
        compiler_params=pltpu.CompilerParams(vmem_limit_bytes=POINTS_VMEM),
        name="points_pass",
    )(in_hbm(snapshots), *pairs, *[in_hbm(a.reshape(1, count)) for a in (observed, precision)], basis)


def tile_at(n):
    return pl.ds(pl.multiple_of(n * 8, 8), 8)


def factor_and_solve(sys_ref, panel_ref, wide_ref, rhs_ref, out_ref):
    tiles = R // 8
    sub = lax.broadcasted_iota(jnp.int32, (8, R), 0)

    def row_of(ref, k, row):
        return jnp.broadcast_to(ref[k, pl.ds(row, 1), :], (8, R))

    def in_one_tile(rows):
        out = rows[0]
        for k in range(1, 8):
            out = jnp.where(sub == k, rows[k], out)
        return out

    def panel(p, base):
        first = p * 8
        corner = [[row_of(sys_ref, first + k, first + i) if i >= k else None for k in range(8)] for i in range(8)]
        low = [[None] * 8 for _ in range(8)]
        inverse = [None] * 8
        for k in range(8):
            inverse[k] = 1.0 / corner[k][k]
            for i in range(k + 1, 8):
                low[i][k] = corner[i][k] * inverse[k]
            for j in range(k + 1, 8):
                for i in range(j, 8):
                    corner[i][j] = corner[i][j] - corner[i][k] * low[j][k]
        y = [jnp.broadcast_to(rhs_ref[pl.ds(first + k, 1), :], (8, R)) for k in range(8)]
        for k in range(8):
            for m in range(k):
                y[k] = y[k] - low[k][m] * y[m]
        out_ref[tile_at(p), :] = in_one_tile([y[k] * inverse[k] for k in range(8)])

        def below(t, carry):
            at = tile_at(t)
            columns = [sys_ref[first + k, at, :] for k in range(8)]
            rhs = rhs_ref[at, :]
            for k in range(8):
                for m in range(k):
                    columns[k] = columns[k] - columns[m] * low[k][m]
                panel_ref[base + k, at, :] = columns[k]
                factor = columns[k] * inverse[k]
                sys_ref[first + k, at, :] = factor
                for r in range(8):
                    wide_ref[t * 8 + r, base + k] = jnp.broadcast_to(factor[r : r + 1], (8, R))
                rhs = rhs - factor * y[k]
            rhs_ref[at, :] = rhs
            return carry

        lax.fori_loop(p, tiles, below, 0)

    def update(depth, size, tj, start, h, carry):
        at = [tile_at(start + size * h + e) for e in range(size)]
        for j in range(8):
            row = tj * 8 + j
            total = [sys_ref[row, at[e], :] for e in range(size)]
            for k in range(depth):
                factor = wide_ref[row, k]
                for e in range(size):
                    total[e] = total[e] - panel_ref[k, at[e], :] * factor
            for e in range(size):
                sys_ref[row, at[e], :] = total[e]
        return carry

    def two_panels(q, carry):
        p = 2 * q
        panel(p, 0)
        lax.fori_loop(p + 1, tiles, functools.partial(update, 8, 1, p + 1, 0), 0)
        panel(p + 1, 8)

        def trailing(tj, carry):
            odd = (tiles - tj) % 2
            lax.fori_loop(0, odd, functools.partial(update, 16, 1, tj, tj), carry)
            return lax.fori_loop(0, (tiles - tj) // 2, functools.partial(update, 16, 2, tj, tj + odd), carry)

        return lax.fori_loop(p + 2, tiles, trailing, carry)

    lax.fori_loop(0, tiles // 2, two_panels, 0)

    def back(n, carry):
        p = tiles - 1 - n
        first = p * 8

        def gather(t, sums):
            at = tile_at(t)
            x = out_ref[at, :]
            return tuple(sums[k] + sys_ref[first + k, at, :] * x for k in range(8))

        sums = lax.fori_loop(p + 1, tiles, gather, tuple(jnp.zeros((8, R), f32) for _ in range(8)))
        x = [
            jnp.broadcast_to(out_ref[pl.ds(first + k, 1), :] - jnp.sum(sums[k], axis=0, keepdims=True), (8, R))
            for k in range(8)
        ]
        for k in range(7, 0, -1):
            for m in range(k):
                x[m] = x[m] - row_of(sys_ref, first + m, first + k) * x[k]
        out_ref[tile_at(p), :] = in_one_tile(x)
        return carry

    lax.fori_loop(0, tiles, back, 0)


def in_three(x):
    high = x.astype(bf16).astype(f32)
    middle = (x - high).astype(bf16).astype(f32)
    return high, middle, x - high - middle


def steps_kernel(picks_ref, gathered_ref, mine_ref, other_ref, out_ref,
                 sums_ref, sys_ref, panel_ref, wide_ref, rhs_ref, step_ref):
    scale = R / PTS
    core, dom = lax.axis_index(C), lax.axis_index(DOM)
    for half in range(2):

        @pl.when(core == half)
        def _():
            sums_ref[half * HALF : (half + 1) * HALF, :] = mine_ref[...]
            sums_ref[(1 - half) * HALF : (2 - half) * HALF, :] = other_ref[...]

    lane = lax.broadcasted_iota(jnp.int32, (8, R), 1)
    sub = lax.broadcasted_iota(jnp.int32, (8, R), 0)
    square_r = lax.broadcasted_iota(jnp.int32, (R, R), 0)
    square_q = lax.broadcasted_iota(jnp.int32, (R, R), 1)
    eye = (square_r == square_q).astype(f32)

    everyone = particles(gathered_ref)
    tags = [gathered_ref[d, NP_DEV : NP_DEV + 1, :] for d in range(N_DOM)]
    first_half = lane[0:1] < NP_DEV
    counts = jnp.concatenate(
        [jnp.where(first_half, tags[d], pltpu.roll(tags[d + 1], NP_DEV, 1)) for d in range(0, N_DOM, 2)], axis=1
    )

    owners = pltpu.roll(jnp.concatenate(tags, axis=0), NP_DEV, 1)
    named = jnp.where((owners == dom.astype(f32)) & (lane < NP_DEV), 1.0, 0.0)
    before = jnp.dot(named, (square_r < square_q).astype(f32), precision=highest, preferred_element_type=f32)
    slot = lax.broadcasted_iota(jnp.int32, (16, R), 0).astype(f32)
    own, valid = [], []
    for d in range(N_DOM):
        choose = jnp.where((named[d : d + 1] > 0.5) & (before[d : d + 1] == slot), 1.0, 0.0)
        valid.append(jnp.sum(choose, axis=1, keepdims=True))
        own.append(jnp.dot(choose[:, :NP_DEV], gathered_ref[d, 0:NP_DEV, :], precision=highest,
                           preferred_element_type=f32))
    own, valid = jnp.concatenate(own, axis=0), jnp.concatenate(valid, axis=0)

    mean_hess = sums_ref[NPART : NPART + R, :]
    for s in range(1, SNAP):
        mean_hess = mean_hess + sums_ref[NPART + s * R : NPART + (s + 1) * R, :]
    mean_hess = eye + mean_hess * (scale / SNAP)
    trace = jnp.sum(jnp.sum(mean_hess * eye, axis=1, keepdims=True), axis=0, keepdims=True)
    repulse = 6.0 / trace

    lifted = jnp.dot(everyone, mean_hess, precision=highest, preferred_element_type=f32)
    ones = jnp.ones((8, R), f32)
    norms = lax.dot_general(ones, lifted * everyone, last_pair, precision=highest, preferred_element_type=f32)[0:1]
    own_lift = jnp.dot(own, mean_hess, precision=highest, preferred_element_type=f32)
    own_norm = jnp.sum(own_lift * own, axis=1, keepdims=True)
    cross = lax.dot_general(own_lift, everyone, last_pair, precision=highest, preferred_element_type=f32)
    distance = own_norm + norms - 2.0 * cross
    weights = counts * jnp.exp(-3.0 * distance / trace)
    total = jnp.sum(weights, axis=1, keepdims=True)
    low_weights = weights.astype(bf16)
    carried = (everyone + repulse * lifted).astype(bf16)
    numerator = jnp.dot(low_weights, carried, preferred_element_type=f32)
    grad = jnp.dot(low_weights.astype(f32), sums_ref[0:NPART, :], precision=highest, preferred_element_type=f32)
    drift = -(numerator + scale * grad) / total + repulse * own_lift
    rhs_ref[...] = drift.T

    rows = []
    for s in range(SNAP):
        j = picks_ref[s]
        rows.append(gathered_ref[j // NP_DEV, pl.ds(j % NP_DEV, 1), :])
    rows.append(jnp.zeros((R - SNAP, R), f32))
    picked = jnp.concatenate(rows, axis=0)
    picked_lift = jnp.dot(picked, mean_hess, precision=highest, preferred_element_type=f32)
    picked_norm = lax.dot_general(ones, picked_lift * picked, last_pair, precision=highest,
                                  preferred_element_type=f32)[0:1]
    picked_cross = lax.dot_general(own_lift, picked, last_pair, precision=highest, preferred_element_type=f32)
    apart = 1.0 + (own_norm + picked_norm - 2.0 * picked_cross) / trace
    mixture = jnp.where(square_q < SNAP, 1.0 / (apart * apart), 0.0)
    mixture = mixture / jnp.sum(mixture, axis=1, keepdims=True)
    shares = mixture.T[0:SNAP, :]
    share_sum = jnp.sum(shares, axis=0, keepdims=True)
    high, middle, low = in_three(shares * scale)
    factors = jnp.concatenate([high, middle, low, high, middle, high], axis=0).astype(bf16)

    def assemble(g, carry):
        parts = []
        for k in range(8):
            hess_rows = sums_ref[pl.ds(NPART + g * 8 + k, SNAP, stride=R), :]
            high, middle, low = in_three(hess_rows)
            parts.append(jnp.concatenate([high, high, high, middle, middle, low], axis=0).astype(bf16))
        product = lax.dot_general(jnp.concatenate(parts, axis=1), factors, (((0,), (0,)), ((), ())),
                                  preferred_element_type=f32)
        for k in range(8):
            sys_ref[g * 8 + k] = product[k * R : (k + 1) * R]
            sys_ref[g * 8 + k, tile_at(g), :] += jnp.where(sub == k, share_sum, 0.0)
        return carry

    lax.fori_loop(0, R // 8, assemble, 0, unroll=8)
    factor_and_solve(sys_ref, panel_ref, wide_ref, rhs_ref, step_ref)
    out_ref[...] = jnp.where(valid > 0.5, own + step_ref[...].T, 0.0)


def newton_rows(snapshots, gathered, mine, other):
    vmem = pl.BlockSpec(memory_space=pltpu.VMEM)
    smem = pl.BlockSpec(memory_space=pltpu.SMEM)
    return pl.pallas_call(
        steps_kernel,
        out_shape=jax.ShapeDtypeStruct((R, R), f32),
        in_specs=[smem, vmem, vmem, vmem],
        out_specs=vmem,
        scratch_shapes=[
            pltpu.VMEM((ROWS, R), f32),
            pltpu.VMEM((R, R, R), f32),
            pltpu.VMEM((16, R, R), f32),
            pltpu.VMEM((R, 16, 8, R), f32),
            pltpu.VMEM((R, R), f32),
            pltpu.VMEM((R, R), f32),
        ],
        compiler_params=pltpu.CompilerParams(vmem_limit_bytes=STEPS_VMEM),
        name="newton_rows",
    )(snapshots, gathered, mine, other)


def sent_to_all(shard, axes):
    copies = jnp.broadcast_to(shard, (lax.axis_size(axes), *shard.shape))
    return lax.all_to_all(copies, axes, split_axis=0, concat_axis=0, tiled=True)


def body(coefficients, copies, owner, snapshots, basis, observed, precision):
    swap = [(0, 1), (1, 0)]
    lines = packed_lines(coefficients, copies, owner)
    pair = lax.all_gather(lines, C, axis=0, tiled=True)
    pairs = [pair] + [lax.ppermute(pair, Y, [(y, (y + shift) % 4) for y in range(4)]) for shift in (1, 2, 3)]
    gathered, keep, send = points_pass(snapshots, pairs, observed, precision, basis)
    part = keep + lax.ppermute(send, C, swap)
    chips = lax.axis_size(CHIPS)
    blocks = lax.all_to_all(part.reshape(chips, HALF // chips, R), CHIPS, 0, 0, tiled=True)
    mine = sent_to_all(jnp.sum(blocks, axis=0), CHIPS).reshape(HALF, R)
    other = lax.ppermute(mine, C, swap)
    rows = newton_rows(snapshots, gathered, mine, other)
    return rows.reshape(1, N_DOM, 2 * NP_DEV // N_DOM, R)


def solution(mesh):
    finer = Mesh(mesh.devices.reshape(4, 4, 4, 2), FIELD_DOM)
    return jax.shard_map(
        body,
        mesh=finer,
        in_specs=(
            P(DOM, None),
            P(DOM),
            P(DOM, None),
            P(),
            P(FIELD_DOM, None),
            P(FIELD_DOM),
            P(FIELD_DOM),
        ),
        out_specs=P(DOM, None, None, None),
        check_vma=False,
    )
```

```python
import functools

import jax
import jax.numpy as jnp
from jax import lax
from jax.experimental import pallas as pl
from jax.experimental.pallas import tpu as pltpu
from jax.sharding import Mesh
from jax.sharding import PartitionSpec as P

PTS = 4194304
R = 128
NP_DEV = 64
NPART = 512
SNAP = 8
N_DOM = 8
ROWS = NPART + SNAP * R
HALF = ROWS // 2
LINES = 72
X, Z, Y, C = "field_0", "field_1", "dom_0", "dom_1"
DOM = (Y, C)
FIELD = (X, Z)
CHIPS = (X, Z, Y)
FIELD_DOM = (X, Z, Y, C)
f32, bf16 = jnp.float32, jnp.bfloat16
highest = lax.Precision.HIGHEST
last_pair = (((1,), (1,)), ((), ()))
POINTS_VMEM = 51 << 20
STEPS_VMEM = 30 << 20


def lines_kernel(coef_ref, copies_ref, owner_ref, lines_ref):
    lines_ref[0:NP_DEV, :] = coef_ref[...]
    tags = jnp.concatenate([copies_ref[...], owner_ref[...]], axis=1).astype(f32)
    lines_ref[NP_DEV:LINES, :] = jnp.broadcast_to(tags, (LINES - NP_DEV, R))


def packed_lines(coefficients, copies, owner):
    return pl.pallas_call(
        lines_kernel,
        out_shape=jax.ShapeDtypeStruct((LINES, R), f32),
        compiler_params=pltpu.CompilerParams(vmem_limit_bytes=60 << 20),
        name="packed_lines",
    )(coefficients, copies.reshape(1, NP_DEV), owner.reshape(1, NP_DEV))


def in_three(x):
    high = x.astype(bf16).astype(f32)
    middle = (x - high).astype(bf16).astype(f32)
    return high, middle, x - high - middle


def particles(gathered_ref):
    return jnp.concatenate([gathered_ref[d, 0:NP_DEV, :] for d in range(N_DOM)], axis=0)


def points_kernel(block, chunk, picks_ref, near_ref, one_ref, two_ref, three_ref, obs_ref, prec_ref, basis_ref,
                  gathered_ref, keep_ref, send_ref, coef_ref, pick_ref, sums_ref, left_ref, right_ref):
    step = pl.program_id(0)

    @pl.when(step == 0)
    def _():
        sums_ref[...] = jnp.zeros_like(sums_ref)
        y = lax.axis_index(Y)
        for shift, pair_ref in enumerate((near_ref, one_ref, two_ref, three_ref)):
            for j in range(2):
                source = (y + 4 - shift) % 4 * 2 + j
                gathered_ref[source] = pair_ref[j * LINES : (j + 1) * LINES, :]
        coef_ref[0:R, :] = particles(gathered_ref).astype(bf16).T
        minus = lax.broadcasted_iota(jnp.int32, (R, NPART), 0) < 3
        coef_ref[R : 2 * R, :] = jnp.where(minus, -1.0, 0.0).astype(bf16)
        rows = []
        for s in range(SNAP):
            j = picks_ref[s]
            rows.append(gathered_ref[j // NP_DEV, pl.ds(j % NP_DEV, 1), :])
        rows.append(jnp.zeros((SNAP, R), f32))
        pick_ref[...] = jnp.concatenate(rows, axis=0).astype(bf16)

    for c in range(block // chunk):
        at = pl.ds(c * chunk, chunk)
        rows = basis_ref[at, :]
        columns = rows.T
        observed = obs_ref[:, at]
        left_ref[:, at] = (columns.astype(f32) * prec_ref[:, at]).astype(bf16)
        picked = jnp.dot(pick_ref[...], columns, preferred_element_type=f32)[0:SNAP]
        slopes = jnp.tanh(picked - observed)
        bend = (1.0 - slopes * slopes).astype(bf16)
        terms = jnp.concatenate([*in_three(observed), jnp.zeros((13, chunk), f32)], axis=0).astype(bf16)
        terms = jnp.concatenate([terms, jnp.zeros((R - 16, chunk), bf16)], axis=0).T
        field = jnp.dot(jnp.concatenate([rows, terms], axis=1), coef_ref[...], preferred_element_type=f32)
        right_ref[at, 0:NPART] = jnp.tanh(field).astype(bf16)
        for s in range(SNAP):
            first = NPART + s * R
            right_ref[at, first : first + R] = (bend[s : s + 1, :] * columns).T
    sums_ref[...] += jnp.dot(left_ref[...], right_ref[...], preferred_element_type=f32)

    @pl.when(step == pl.num_programs(0) - 1)
    def _():
        for core in range(2):

            @pl.when(lax.axis_index(C) == core)
            def _():
                for half, part_ref in ((core, keep_ref), (1 - core, send_ref)):
                    for k in range(HALF // R):
                        first = half * HALF + k * R
                        part_ref[k * R : (k + 1) * R, :] = sums_ref[:, first : first + R]


def in_hbm(x):
    return pltpu.with_memory_space_constraint(x, pltpu.HBM)


def points_pass(snapshots, pairs, observed, precision, basis):
    block, chunk = 4096, 256
    count = basis.shape[0]
    whole = lambda i, *_: (0, 0)
    return pl.pallas_call(
        functools.partial(points_kernel, block, chunk),
        out_shape=[jax.ShapeDtypeStruct((N_DOM, LINES, R), f32)] + [jax.ShapeDtypeStruct((HALF, R), f32)] * 2,
        grid_spec=pltpu.PrefetchScalarGridSpec(
            num_scalar_prefetch=1,
            grid=(count // block,),
            in_specs=[
                *[pl.BlockSpec((2 * LINES, R), whole)] * 4,
                pl.BlockSpec((1, block), lambda i, *_: (0, i)),
                pl.BlockSpec((1, block), lambda i, *_: (0, i)),
                pl.BlockSpec((block, R), lambda i, *_: (i, 0)),
            ],
            out_specs=[pl.BlockSpec((N_DOM, LINES, R), lambda i, *_: (0, 0, 0))] + [pl.BlockSpec((HALF, R), whole)] * 2,
            scratch_shapes=[
                pltpu.VMEM((2 * R, NPART), bf16),
                pltpu.VMEM((16, R), bf16),
                pltpu.VMEM((R, ROWS), f32),
                pltpu.VMEM((R, block), bf16),
                pltpu.VMEM((block, ROWS), bf16),
            ],
        ),
        compiler_params=pltpu.CompilerParams(vmem_limit_bytes=POINTS_VMEM),
        name="points_pass",
    )(in_hbm(snapshots), *pairs, *[in_hbm(a.reshape(1, count)) for a in (observed, precision)], basis)


def tile_at(n):
    return pl.ds(pl.multiple_of(n * 8, 8), 8)


def factor_and_solve(sys_ref, panel_ref, wide_ref, rhs_ref, out_ref):
    tiles = R // 8
    sub = lax.broadcasted_iota(jnp.int32, (8, R), 0)

    def row_of(ref, k, row):
        return jnp.broadcast_to(ref[k, pl.ds(row, 1), :], (8, R))

    def in_one_tile(rows):
        out = rows[0]
        for k in range(1, 8):
            out = jnp.where(sub == k, rows[k], out)
        return out

    def panel(p, base):
        first = p * 8
        corner = [[row_of(sys_ref, first + k, first + i) if i >= k else None for k in range(8)] for i in range(8)]
        low = [[None] * 8 for _ in range(8)]
        inverse = [None] * 8
        for k in range(8):
            inverse[k] = 1.0 / corner[k][k]
            for i in range(k + 1, 8):
                low[i][k] = corner[i][k] * inverse[k]
            for j in range(k + 1, 8):
                for i in range(j, 8):
                    corner[i][j] = corner[i][j] - corner[i][k] * low[j][k]
        y = [jnp.broadcast_to(rhs_ref[pl.ds(first + k, 1), :], (8, R)) for k in range(8)]
        for k in range(8):
            for m in range(k):
                y[k] = y[k] - low[k][m] * y[m]
        out_ref[tile_at(p), :] = in_one_tile([y[k] * inverse[k] for k in range(8)])

        def below(t, carry):
            at = tile_at(t)
            columns = [sys_ref[first + k, at, :] for k in range(8)]
            rhs = rhs_ref[at, :]
            for k in range(8):
                for m in range(k):
                    columns[k] = columns[k] - columns[m] * low[k][m]
                panel_ref[base + k, at, :] = columns[k]
                factor = columns[k] * inverse[k]
                sys_ref[first + k, at, :] = factor
                for r in range(8):
                    wide_ref[t * 8 + r, base + k] = jnp.broadcast_to(factor[r : r + 1], (8, R))
                rhs = rhs - factor * y[k]
            rhs_ref[at, :] = rhs
            return carry

        lax.fori_loop(p, tiles, below, 0)

    def update(depth, size, tj, start, h, carry):
        at = [tile_at(start + size * h + e) for e in range(size)]
        for j in range(8):
            row = tj * 8 + j
            total = [sys_ref[row, at[e], :] for e in range(size)]
            for k in range(depth):
                factor = wide_ref[row, k]
                for e in range(size):
                    total[e] = total[e] - panel_ref[k, at[e], :] * factor
            for e in range(size):
                sys_ref[row, at[e], :] = total[e]
        return carry

    def two_panels(q, carry):
        p = 2 * q
        panel(p, 0)
        lax.fori_loop(p + 1, tiles, functools.partial(update, 8, 1, p + 1, 0), 0)
        panel(p + 1, 8)

        def trailing(tj, carry):
            odd = (tiles - tj) % 2
            lax.fori_loop(0, odd, functools.partial(update, 16, 1, tj, tj), carry)
            return lax.fori_loop(0, (tiles - tj) // 2, functools.partial(update, 16, 2, tj, tj + odd), carry)

        return lax.fori_loop(p + 2, tiles, trailing, carry)

    lax.fori_loop(0, tiles // 2, two_panels, 0)

    def back(n, carry):
        p = tiles - 1 - n
        first = p * 8

        def gather(t, sums):
            at = tile_at(t)
            x = out_ref[at, :]
            return tuple(sums[k] + sys_ref[first + k, at, :] * x for k in range(8))

        sums = lax.fori_loop(p + 1, tiles, gather, tuple(jnp.zeros((8, R), f32) for _ in range(8)))
        x = [
            jnp.broadcast_to(out_ref[pl.ds(first + k, 1), :] - jnp.sum(sums[k], axis=0, keepdims=True), (8, R))
            for k in range(8)
        ]
        for k in range(7, 0, -1):
            for m in range(k):
                x[m] = x[m] - row_of(sys_ref, first + m, first + k) * x[k]
        out_ref[tile_at(p), :] = in_one_tile(x)
        return carry

    lax.fori_loop(0, tiles, back, 0)


def steps_kernel(picks_ref, gathered_ref, mine_ref, other_ref, out_ref,
                 sums_ref, sys_ref, panel_ref, wide_ref, rhs_ref, step_ref):
    scale = R / PTS
    core, dom = lax.axis_index(C), lax.axis_index(DOM)
    for half in range(2):

        @pl.when(core == half)
        def _():
            sums_ref[half * HALF : (half + 1) * HALF, :] = mine_ref[...]
            sums_ref[(1 - half) * HALF : (2 - half) * HALF, :] = other_ref[...]

    lane = lax.broadcasted_iota(jnp.int32, (8, R), 1)
    sub = lax.broadcasted_iota(jnp.int32, (8, R), 0)
    square_r = lax.broadcasted_iota(jnp.int32, (R, R), 0)
    square_q = lax.broadcasted_iota(jnp.int32, (R, R), 1)
    eye = (square_r == square_q).astype(f32)

    everyone = particles(gathered_ref)
    tags = [gathered_ref[d, NP_DEV : NP_DEV + 1, :] for d in range(N_DOM)]
    first_half = lane[0:1] < NP_DEV
    counts = jnp.concatenate(
        [jnp.where(first_half, tags[d], pltpu.roll(tags[d + 1], NP_DEV, 1)) for d in range(0, N_DOM, 2)], axis=1
    )

    owners = pltpu.roll(jnp.concatenate(tags, axis=0), NP_DEV, 1)
    named = jnp.where((owners == dom.astype(f32)) & (lane < NP_DEV), 1.0, 0.0)
    before = jnp.dot(named, (square_r < square_q).astype(f32), precision=highest, preferred_element_type=f32)
    slot = lax.broadcasted_iota(jnp.int32, (16, R), 0).astype(f32)
    own, valid = [], []
    for d in range(N_DOM):
        choose = jnp.where((named[d : d + 1] > 0.5) & (before[d : d + 1] == slot), 1.0, 0.0)
        valid.append(jnp.sum(choose, axis=1, keepdims=True))
        own.append(jnp.dot(choose[:, :NP_DEV], gathered_ref[d, 0:NP_DEV, :], precision=highest,
                           preferred_element_type=f32))
    own, valid = jnp.concatenate(own, axis=0), jnp.concatenate(valid, axis=0)

    mean_hess = sums_ref[NPART : NPART + R, :]
    for s in range(1, SNAP):
        mean_hess = mean_hess + sums_ref[NPART + s * R : NPART + (s + 1) * R, :]
    mean_hess = eye + mean_hess * (scale / SNAP)
    trace = jnp.sum(jnp.sum(mean_hess * eye, axis=1, keepdims=True), axis=0, keepdims=True)
    repulse = 6.0 / trace

    lifted = jnp.dot(everyone, mean_hess, precision=highest, preferred_element_type=f32)
    ones = jnp.ones((8, R), f32)
    norms = lax.dot_general(ones, lifted * everyone, last_pair, precision=highest, preferred_element_type=f32)[0:1]
    own_lift = jnp.dot(own, mean_hess, precision=highest, preferred_element_type=f32)
    own_norm = jnp.sum(own_lift * own, axis=1, keepdims=True)
    cross = lax.dot_general(own_lift, everyone, last_pair, precision=highest, preferred_element_type=f32)
    distance = own_norm + norms - 2.0 * cross
    weights = counts * jnp.exp(-3.0 * distance / trace)
    total = jnp.sum(weights, axis=1, keepdims=True)
    low_weights = weights.astype(bf16)
    carried = (everyone + repulse * lifted).astype(bf16)
    numerator = jnp.dot(low_weights, carried, preferred_element_type=f32)
    rounded = low_weights.astype(f32)
    grad = jnp.zeros((R, R), f32)
    for k in range(0, NPART, R):
        grad = grad + lax.dot_general(rounded[:, k : k + R], sums_ref[k : k + R, :], last_pair, precision=highest,
                                      preferred_element_type=f32)
    drift = -(numerator + scale * grad) / total + repulse * own_lift
    rhs_ref[...] = drift.T

    rows = []
    for s in range(SNAP):
        j = picks_ref[s]
        rows.append(gathered_ref[j // NP_DEV, pl.ds(j % NP_DEV, 1), :])
    rows.append(jnp.zeros((R - SNAP, R), f32))
    picked = jnp.concatenate(rows, axis=0)
    picked_lift = jnp.dot(picked, mean_hess, precision=highest, preferred_element_type=f32)
    picked_norm = lax.dot_general(ones, picked_lift * picked, last_pair, precision=highest,
                                  preferred_element_type=f32)[0:1]
    picked_cross = lax.dot_general(own_lift, picked, last_pair, precision=highest, preferred_element_type=f32)
    apart = 1.0 + (own_norm + picked_norm - 2.0 * picked_cross) / trace
    mixture = jnp.where(square_q < SNAP, 1.0 / (apart * apart), 0.0)
    mixture = mixture / jnp.sum(mixture, axis=1, keepdims=True)
    shares = mixture.T[0:SNAP, :]
    share_sum = jnp.sum(shares, axis=0, keepdims=True)
    high, middle, low = in_three(shares * scale)
    factors = jnp.concatenate([high, middle, low, high, middle, high], axis=0).astype(bf16)

    def assemble(g, carry):
        parts = []
        for k in range(8):
            hess_rows = sums_ref[pl.ds(NPART + g * 8 + k, SNAP, stride=R), :]
            high, middle, low = in_three(hess_rows)
            parts.append(jnp.concatenate([high, high, high, middle, middle, low], axis=0).astype(bf16))
        product = lax.dot_general(jnp.concatenate(parts, axis=1), factors, (((0,), (0,)), ((), ())),
                                  preferred_element_type=f32)
        for k in range(8):
            sys_ref[g * 8 + k] = product[k * R : (k + 1) * R]
            sys_ref[g * 8 + k, tile_at(g), :] += jnp.where(sub == k, share_sum, 0.0)
        return carry

    lax.fori_loop(0, R // 8, assemble, 0, unroll=8)
    factor_and_solve(sys_ref, panel_ref, wide_ref, rhs_ref, step_ref)
    out_ref[...] = jnp.where(valid > 0.5, own + step_ref[...].T, 0.0)


def newton_rows(snapshots, gathered, mine, other):
    vmem = pl.BlockSpec(memory_space=pltpu.VMEM)
    smem = pl.BlockSpec(memory_space=pltpu.SMEM)
    return pl.pallas_call(
        steps_kernel,
        out_shape=jax.ShapeDtypeStruct((R, R), f32),
        in_specs=[smem, vmem, vmem, vmem],
        out_specs=vmem,
        scratch_shapes=[
            pltpu.VMEM((ROWS, R), f32),
            pltpu.VMEM((R, R, R), f32),
            pltpu.VMEM((16, R, R), f32),
            pltpu.VMEM((R, 16, 8, R), f32),
            pltpu.VMEM((R, R), f32),
            pltpu.VMEM((R, R), f32),
        ],
        compiler_params=pltpu.CompilerParams(vmem_limit_bytes=STEPS_VMEM),
        name="newton_rows",
    )(snapshots, gathered, mine, other)


def sent_to_all(shard, axes):
    copies = jnp.broadcast_to(shard, (lax.axis_size(axes), *shard.shape))
    return lax.all_to_all(copies, axes, split_axis=0, concat_axis=0, tiled=True)


def body(coefficients, copies, owner, snapshots, basis, observed, precision):
    swap = [(0, 1), (1, 0)]
    lines = packed_lines(coefficients, copies, owner)
    pair = lax.all_gather(lines, C, axis=0, tiled=True)
    pairs = [pair] + [lax.ppermute(pair, Y, [(y, (y + shift) % 4) for y in range(4)]) for shift in (1, 2, 3)]
    gathered, keep, send = points_pass(snapshots, pairs, observed, precision, basis)
    part = keep + lax.ppermute(send, C, swap)
    chips = lax.axis_size(CHIPS)
    blocks = lax.all_to_all(part.reshape(chips, HALF // chips, R), CHIPS, 0, 0, tiled=True)
    mine = sent_to_all(jnp.sum(blocks, axis=0), CHIPS).reshape(HALF, R)
    other = lax.ppermute(mine, C, swap)
    rows = newton_rows(snapshots, gathered, mine, other)
    return rows.reshape(1, N_DOM, 2 * NP_DEV // N_DOM, R)


def solution(mesh):
    finer = Mesh(mesh.devices.reshape(4, 4, 4, 2), FIELD_DOM)
    return jax.shard_map(
        body,
        mesh=finer,
        in_specs=(
            P(DOM, None),
            P(DOM),
            P(DOM, None),
            P(),
            P(FIELD_DOM, None),
            P(FIELD_DOM),
            P(FIELD_DOM),
        ),
        out_specs=P(DOM, None, None, None),
        check_vma=False,
    )
```

```python
import functools

import jax
import jax.numpy as jnp
from jax import lax
from jax.experimental import pallas as pl
from jax.experimental.pallas import tpu as pltpu
from jax.sharding import Mesh
from jax.sharding import PartitionSpec as P

PTS = 4194304
R = 128
NP_DEV = 64
NPART = 512
SNAP = 8
N_DOM = 8
ROWS = NPART + SNAP * R
HALF = ROWS // 2
LINES = 72
X, Z, Y, C = "field_0", "field_1", "dom_0", "dom_1"
DOM = (Y, C)
FIELD = (X, Z)
CHIPS = (X, Z, Y)
FIELD_DOM = (X, Z, Y, C)
f32, bf16 = jnp.float32, jnp.bfloat16
highest = lax.Precision.HIGHEST
last_pair = (((1,), (1,)), ((), ()))
POINTS_VMEM = 51 << 20
STEPS_VMEM = 30 << 20


def lines_kernel(coef_ref, copies_ref, owner_ref, lines_ref):
    lines_ref[0:NP_DEV, :] = coef_ref[...]
    tags = jnp.concatenate([copies_ref[...], owner_ref[...]], axis=1).astype(f32)
    lines_ref[NP_DEV:LINES, :] = jnp.broadcast_to(tags, (LINES - NP_DEV, R))


def packed_lines(coefficients, copies, owner):
    return pl.pallas_call(
        lines_kernel,
        out_shape=jax.ShapeDtypeStruct((LINES, R), f32),
        compiler_params=pltpu.CompilerParams(vmem_limit_bytes=60 << 20),
        name="packed_lines",
    )(coefficients, copies.reshape(1, NP_DEV), owner.reshape(1, NP_DEV))


def in_three(x):
    high = x.astype(bf16).astype(f32)
    middle = (x - high).astype(bf16).astype(f32)
    return high, middle, x - high - middle


def particles(gathered_ref):
    return jnp.concatenate([gathered_ref[d, 0:NP_DEV, :] for d in range(N_DOM)], axis=0)


def points_kernel(block, chunk, picks_ref, near_ref, one_ref, two_ref, three_ref, obs_ref, prec_ref, basis_ref,
                  gathered_ref, keep_ref, send_ref, coef_ref, pick_ref, sums_ref, left_ref, right_ref):
    step = pl.program_id(0)

    @pl.when(step == 0)
    def _():
        sums_ref[...] = jnp.zeros_like(sums_ref)
        y = lax.axis_index(Y)
        for shift, pair_ref in enumerate((near_ref, one_ref, two_ref, three_ref)):
            for j in range(2):
                source = (y + 4 - shift) % 4 * 2 + j
                gathered_ref[source] = pair_ref[j * LINES : (j + 1) * LINES, :]
        coef_ref[0:R, :] = particles(gathered_ref).astype(bf16).T
        minus = lax.broadcasted_iota(jnp.int32, (R, NPART), 0) < 3
        coef_ref[R : 2 * R, :] = jnp.where(minus, -1.0, 0.0).astype(bf16)
        rows = []
        for s in range(SNAP):
            j = picks_ref[s]
            rows.append(gathered_ref[j // NP_DEV, pl.ds(j % NP_DEV, 1), :])
        rows.append(jnp.zeros((SNAP, R), f32))
        pick_ref[...] = jnp.concatenate(rows, axis=0).astype(bf16)

    for c in range(block // chunk):
        at = pl.ds(c * chunk, chunk)
        rows = basis_ref[at, :]
        columns = rows.T
        observed = obs_ref[:, at]
        left_ref[:, at] = (columns.astype(f32) * prec_ref[:, at]).astype(bf16)
        picked = jnp.dot(pick_ref[...], columns, preferred_element_type=f32)[0:SNAP]
        slopes = jnp.tanh(picked - observed)
        bend = (1.0 - slopes * slopes).astype(bf16)
        terms = jnp.concatenate([*in_three(observed), jnp.zeros((13, chunk), f32)], axis=0).astype(bf16)
        terms = jnp.concatenate([terms, jnp.zeros((R - 16, chunk), bf16)], axis=0).T
        field = jnp.dot(jnp.concatenate([rows, terms], axis=1), coef_ref[...], preferred_element_type=f32)
        right_ref[at, 0:NPART] = jnp.tanh(field).astype(bf16)
        for s in range(SNAP):
            first = NPART + s * R
            right_ref[at, first : first + R] = (bend[s : s + 1, :] * columns).T
    sums_ref[...] += jnp.dot(left_ref[...], right_ref[...], preferred_element_type=f32)

    @pl.when(step == pl.num_programs(0) - 1)
    def _():
        for core in range(2):

            @pl.when(lax.axis_index(C) == core)
            def _():
                for half, part_ref in ((core, keep_ref), (1 - core, send_ref)):
                    for k in range(HALF // R):
                        first = half * HALF + k * R
                        part_ref[k * R : (k + 1) * R, :] = sums_ref[:, first : first + R]


def in_hbm(x):
    return pltpu.with_memory_space_constraint(x, pltpu.HBM)


def points_pass(snapshots, pairs, observed, precision, basis):
    block, chunk = 4096, 256
    count = basis.shape[0]
    whole = lambda i, *_: (0, 0)
    return pl.pallas_call(
        functools.partial(points_kernel, block, chunk),
        out_shape=[jax.ShapeDtypeStruct((N_DOM, LINES, R), f32)] + [jax.ShapeDtypeStruct((HALF, R), f32)] * 2,
        grid_spec=pltpu.PrefetchScalarGridSpec(
            num_scalar_prefetch=1,
            grid=(count // block,),
            in_specs=[
                *[pl.BlockSpec((2 * LINES, R), whole)] * 4,
                pl.BlockSpec((1, block), lambda i, *_: (0, i)),
                pl.BlockSpec((1, block), lambda i, *_: (0, i)),
                pl.BlockSpec((block, R), lambda i, *_: (i, 0)),
            ],
            out_specs=[pl.BlockSpec((N_DOM, LINES, R), lambda i, *_: (0, 0, 0))] + [pl.BlockSpec((HALF, R), whole)] * 2,
            scratch_shapes=[
                pltpu.VMEM((2 * R, NPART), bf16),
                pltpu.VMEM((16, R), bf16),
                pltpu.VMEM((R, ROWS), f32),
                pltpu.VMEM((R, block), bf16),
                pltpu.VMEM((block, ROWS), bf16),
            ],
        ),
        compiler_params=pltpu.CompilerParams(vmem_limit_bytes=POINTS_VMEM),
        name="points_pass",
    )(in_hbm(snapshots), *pairs, *[in_hbm(a.reshape(1, count)) for a in (observed, precision)], basis)


def tile_at(n):
    return pl.ds(pl.multiple_of(n * 8, 8), 8)


def factor_and_solve(sys_ref, panel_ref, wide_ref, rhs_ref, out_ref):
    tiles = R // 8
    sub = lax.broadcasted_iota(jnp.int32, (8, R), 0)

    def row_of(ref, k, row):
        return jnp.broadcast_to(ref[k, pl.ds(row, 1), :], (8, R))

    def in_one_tile(rows):
        out = rows[0]
        for k in range(1, 8):
            out = jnp.where(sub == k, rows[k], out)
        return out

    def panel(p, base):
        first = p * 8
        corner = [[row_of(sys_ref, first + k, first + i) if i >= k else None for k in range(8)] for i in range(8)]
        low = [[None] * 8 for _ in range(8)]
        inverse = [None] * 8
        for k in range(8):
            inverse[k] = 1.0 / corner[k][k]
            for i in range(k + 1, 8):
                low[i][k] = corner[i][k] * inverse[k]
            for j in range(k + 1, 8):
                for i in range(j, 8):
                    corner[i][j] = corner[i][j] - corner[i][k] * low[j][k]
        y = [jnp.broadcast_to(rhs_ref[pl.ds(first + k, 1), :], (8, R)) for k in range(8)]
        for k in range(8):
            for m in range(k):
                y[k] = y[k] - low[k][m] * y[m]
        out_ref[tile_at(p), :] = in_one_tile([y[k] * inverse[k] for k in range(8)])

        def below(t, carry):
            at = tile_at(t)
            columns = [sys_ref[first + k, at, :] for k in range(8)]
            rhs = rhs_ref[at, :]
            for k in range(8):
                for m in range(k):
                    columns[k] = columns[k] - columns[m] * low[k][m]
                panel_ref[base + k, at, :] = columns[k]
                factor = columns[k] * inverse[k]
                sys_ref[first + k, at, :] = factor
                for r in range(8):
                    wide_ref[t * 8 + r, base + k] = jnp.broadcast_to(factor[r : r + 1], (8, R))
                rhs = rhs - factor * y[k]
            rhs_ref[at, :] = rhs
            return carry

        lax.fori_loop(p, tiles, below, 0)

    def update(depth, size, tj, start, h, carry):
        at = [tile_at(start + size * h + e) for e in range(size)]
        for j in range(8):
            row = tj * 8 + j
            total = [sys_ref[row, at[e], :] for e in range(size)]
            for k in range(depth):
                factor = wide_ref[row, k]
                for e in range(size):
                    total[e] = total[e] - panel_ref[k, at[e], :] * factor
            for e in range(size):
                sys_ref[row, at[e], :] = total[e]
        return carry

    def two_panels(q, carry):
        p = 2 * q
        panel(p, 0)
        lax.fori_loop(p + 1, tiles, functools.partial(update, 8, 1, p + 1, 0), 0)
        panel(p + 1, 8)

        def trailing(tj, carry):
            odd = (tiles - tj) % 2
            lax.fori_loop(0, odd, functools.partial(update, 16, 1, tj, tj), carry)
            return lax.fori_loop(0, (tiles - tj) // 2, functools.partial(update, 16, 2, tj, tj + odd), carry)

        return lax.fori_loop(p + 2, tiles, trailing, carry)

    lax.fori_loop(0, tiles // 2, two_panels, 0)

    def back(n, carry):
        p = tiles - 1 - n
        first = p * 8

        def gather(t, sums):
            at = tile_at(t)
            x = out_ref[at, :]
            return tuple(sums[k] + sys_ref[first + k, at, :] * x for k in range(8))

        sums = lax.fori_loop(p + 1, tiles, gather, tuple(jnp.zeros((8, R), f32) for _ in range(8)))
        x = [
            jnp.broadcast_to(out_ref[pl.ds(first + k, 1), :] - jnp.sum(sums[k], axis=0, keepdims=True), (8, R))
            for k in range(8)
        ]
        for k in range(7, 0, -1):
            for m in range(k):
                x[m] = x[m] - row_of(sys_ref, first + m, first + k) * x[k]
        out_ref[tile_at(p), :] = in_one_tile(x)
        return carry

    lax.fori_loop(0, tiles, back, 0)


def steps_kernel(picks_ref, gathered_ref, mine_ref, other_ref, out_ref,
                 sums_ref, sys_ref, panel_ref, wide_ref, rhs_ref, step_ref):
    scale = R / PTS
    core, dom = lax.axis_index(C), lax.axis_index(DOM)
    for half in range(2):

        @pl.when(core == half)
        def _():
            sums_ref[half * HALF : (half + 1) * HALF, :] = mine_ref[...]
            sums_ref[(1 - half) * HALF : (2 - half) * HALF, :] = other_ref[...]

    lane = lax.broadcasted_iota(jnp.int32, (8, R), 1)
    sub = lax.broadcasted_iota(jnp.int32, (8, R), 0)
    square_r = lax.broadcasted_iota(jnp.int32, (R, R), 0)
    square_q = lax.broadcasted_iota(jnp.int32, (R, R), 1)
    eye = (square_r == square_q).astype(f32)

    everyone = particles(gathered_ref)
    tags = [gathered_ref[d, NP_DEV : NP_DEV + 1, :] for d in range(N_DOM)]
    first_half = lane[0:1] < NP_DEV
    counts = jnp.concatenate(
        [jnp.where(first_half, tags[d], pltpu.roll(tags[d + 1], NP_DEV, 1)) for d in range(0, N_DOM, 2)], axis=1
    )

    owners = pltpu.roll(jnp.concatenate(tags, axis=0), NP_DEV, 1)
    named = jnp.where((owners == dom.astype(f32)) & (lane < NP_DEV), 1.0, 0.0)
    before = jnp.dot(named, (square_r < square_q).astype(f32), precision=highest, preferred_element_type=f32)
    slot = lax.broadcasted_iota(jnp.int32, (16, R), 0).astype(f32)
    own, valid = [], []
    for d in range(N_DOM):
        choose = jnp.where((named[d : d + 1] > 0.5) & (before[d : d + 1] == slot), 1.0, 0.0)
        valid.append(jnp.sum(choose, axis=1, keepdims=True))
        own.append(jnp.dot(choose[:, :NP_DEV], gathered_ref[d, 0:NP_DEV, :], precision=highest,
                           preferred_element_type=f32))
    own, valid = jnp.concatenate(own, axis=0), jnp.concatenate(valid, axis=0)

    mean_hess = sums_ref[NPART : NPART + R, :]
    for s in range(1, SNAP):
        mean_hess = mean_hess + sums_ref[NPART + s * R : NPART + (s + 1) * R, :]
    mean_hess = eye + mean_hess * (scale / SNAP)
    trace = jnp.sum(jnp.sum(mean_hess * eye, axis=1, keepdims=True), axis=0, keepdims=True)
    repulse = 6.0 / trace

    lifted = jnp.dot(everyone, mean_hess, precision=highest, preferred_element_type=f32)
    ones = jnp.ones((8, R), f32)
    norms = lax.dot_general(ones, lifted * everyone, last_pair, precision=highest, preferred_element_type=f32)[0:1]
    own_lift = jnp.dot(own, mean_hess, precision=highest, preferred_element_type=f32)
    own_norm = jnp.sum(own_lift * own, axis=1, keepdims=True)
    cross = lax.dot_general(own_lift, everyone, last_pair, precision=highest, preferred_element_type=f32)
    distance = own_norm + norms - 2.0 * cross
    weights = counts * jnp.exp(-3.0 * distance / trace)
    total = jnp.sum(weights, axis=1, keepdims=True)
    low_weights = weights.astype(bf16)
    carried = (everyone + repulse * lifted).astype(bf16)
    numerator = jnp.dot(low_weights, carried, preferred_element_type=f32)
    rounded = low_weights.astype(f32)
    grad = jnp.zeros((R, R), f32)
    for k in range(0, NPART, R):
        grad = grad + lax.dot_general(rounded[:, k : k + R], sums_ref[k : k + R, :], last_pair, precision=highest,
                                      preferred_element_type=f32)
    drift = -(numerator + scale * grad) / total + repulse * own_lift
    rhs_ref[...] = drift.T

    rows = []
    for s in range(SNAP):
        j = picks_ref[s]
        rows.append(gathered_ref[j // NP_DEV, pl.ds(j % NP_DEV, 1), :])
    rows.append(jnp.zeros((R - SNAP, R), f32))
    picked = jnp.concatenate(rows, axis=0)
    picked_lift = jnp.dot(picked, mean_hess, precision=highest, preferred_element_type=f32)
    picked_norm = lax.dot_general(ones, picked_lift * picked, last_pair, precision=highest,
                                  preferred_element_type=f32)[0:1]
    picked_cross = lax.dot_general(own_lift, picked, last_pair, precision=highest, preferred_element_type=f32)
    apart = 1.0 + (own_norm + picked_norm - 2.0 * picked_cross) / trace
    mixture = jnp.where(square_q < SNAP, 1.0 / (apart * apart), 0.0)
    mixture = mixture / jnp.sum(mixture, axis=1, keepdims=True)
    shares = mixture.T[0:SNAP, :]
    share_sum = jnp.sum(shares, axis=0, keepdims=True)
    high, middle, low = in_three(shares * scale)
    factors = jnp.concatenate([high, middle, low, high, middle, high], axis=0).astype(bf16)

    def assemble(g, carry):
        parts = []
        for k in range(8):
            hess_rows = sums_ref[pl.ds(NPART + g * 8 + k, SNAP, stride=R), :]
            high, middle, low = in_three(hess_rows)
            parts.append(jnp.concatenate([high, high, high, middle, middle, low], axis=0).astype(bf16))
        product = lax.dot_general(jnp.concatenate(parts, axis=1), factors, (((0,), (0,)), ((), ())),
                                  preferred_element_type=f32)
        for k in range(8):
            sys_ref[g * 8 + k] = product[k * R : (k + 1) * R]
            sys_ref[g * 8 + k, tile_at(g), :] += jnp.where(sub == k, share_sum, 0.0)
        return carry

    lax.fori_loop(0, R // 8, assemble, 0, unroll=8)
    factor_and_solve(sys_ref, panel_ref, wide_ref, rhs_ref, step_ref)
    out_ref[...] = jnp.where(valid > 0.5, own + step_ref[...].T, 0.0)


def newton_rows(snapshots, gathered, mine, other):
    vmem = pl.BlockSpec(memory_space=pltpu.VMEM)
    smem = pl.BlockSpec(memory_space=pltpu.SMEM)
    return pl.pallas_call(
        steps_kernel,
        out_shape=jax.ShapeDtypeStruct((R, R), f32),
        in_specs=[smem, vmem, vmem, vmem],
        out_specs=vmem,
        scratch_shapes=[
            pltpu.VMEM((ROWS + R, R), f32),
            pltpu.VMEM((R, R, R), f32),
            pltpu.VMEM((16, R, R), f32),
            pltpu.VMEM((R, 16, 8, R), f32),
            pltpu.VMEM((R, R), f32),
            pltpu.VMEM((R, R), f32),
        ],
        compiler_params=pltpu.CompilerParams(vmem_limit_bytes=STEPS_VMEM),
        name="newton_rows",
    )(snapshots, gathered, mine, other)


def sent_to_all(shard, axes):
    copies = jnp.broadcast_to(shard, (lax.axis_size(axes), *shard.shape))
    return lax.all_to_all(copies, axes, split_axis=0, concat_axis=0, tiled=True)


def body(coefficients, copies, owner, snapshots, basis, observed, precision):
    swap = [(0, 1), (1, 0)]
    lines = packed_lines(coefficients, copies, owner)
    pair = lax.all_gather(lines, C, axis=0, tiled=True)
    pairs = [pair] + [lax.ppermute(pair, Y, [(y, (y + shift) % 4) for y in range(4)]) for shift in (1, 2, 3)]
    gathered, keep, send = points_pass(snapshots, pairs, observed, precision, basis)
    part = keep + lax.ppermute(send, C, swap)
    chips = lax.axis_size(CHIPS)
    blocks = lax.all_to_all(part.reshape(chips, HALF // chips, R), CHIPS, 0, 0, tiled=True)
    mine = sent_to_all(jnp.sum(blocks, axis=0), CHIPS).reshape(HALF, R)
    other = lax.ppermute(mine, C, swap)
    rows = newton_rows(snapshots, gathered, mine, other)
    return rows.reshape(1, N_DOM, 2 * NP_DEV // N_DOM, R)


def solution(mesh):
    finer = Mesh(mesh.devices.reshape(4, 4, 4, 2), FIELD_DOM)
    return jax.shard_map(
        body,
        mesh=finer,
        in_specs=(
            P(DOM, None),
            P(DOM),
            P(DOM, None),
            P(),
            P(FIELD_DOM, None),
            P(FIELD_DOM),
            P(FIELD_DOM),
        ),
        out_specs=P(DOM, None, None, None),
        check_vma=False,
    )
```

```python
import functools

import jax
import jax.numpy as jnp
from jax import lax
from jax.experimental import pallas as pl
from jax.experimental.pallas import tpu as pltpu
from jax.sharding import Mesh
from jax.sharding import PartitionSpec as P

PTS = 4194304
R = 128
NP_DEV = 64
NPART = 512
SNAP = 8
N_DOM = 8
ROWS = NPART + SNAP * R
HALF = ROWS // 2
LINES = 72
X, Z, Y, C = "field_0", "field_1", "dom_0", "dom_1"
DOM = (Y, C)
FIELD = (X, Z)
CHIPS = (X, Z, Y)
FIELD_DOM = (X, Z, Y, C)
f32, bf16 = jnp.float32, jnp.bfloat16
highest = lax.Precision.HIGHEST
last_pair = (((1,), (1,)), ((), ()))
POINTS_VMEM = 51 << 20
STEPS_VMEM = 30 << 20


def lines_kernel(coef_ref, copies_ref, owner_ref, lines_ref):
    lines_ref[0:NP_DEV, :] = coef_ref[...]
    tags = jnp.concatenate([copies_ref[...], owner_ref[...]], axis=1).astype(f32)
    lines_ref[NP_DEV:LINES, :] = jnp.broadcast_to(tags, (LINES - NP_DEV, R))


def packed_lines(coefficients, copies, owner):
    return pl.pallas_call(
        lines_kernel,
        out_shape=jax.ShapeDtypeStruct((LINES, R), f32),
        compiler_params=pltpu.CompilerParams(vmem_limit_bytes=60 << 20),
        name="packed_lines",
    )(coefficients, copies.reshape(1, NP_DEV), owner.reshape(1, NP_DEV))


def in_three(x):
    high = x.astype(bf16).astype(f32)
    middle = (x - high).astype(bf16).astype(f32)
    return high, middle, x - high - middle


def particles(gathered_ref):
    return jnp.concatenate([gathered_ref[d, 0:NP_DEV, :] for d in range(N_DOM)], axis=0)


def points_kernel(block, chunk, picks_ref, near_ref, one_ref, three_ref, two_ref, obs_ref, prec_ref, basis_ref,
                  gathered_ref, keep_ref, send_ref, coef_ref, pick_ref, sums_ref, left_ref, right_ref):
    step = pl.program_id(0)

    @pl.when(step == 0)
    def _():
        sums_ref[...] = jnp.zeros_like(sums_ref)
        y = lax.axis_index(Y)
        for shift, pair_ref in enumerate((near_ref, one_ref, two_ref, three_ref)):
            for j in range(2):
                source = (y + 4 - shift) % 4 * 2 + j
                gathered_ref[source] = pair_ref[j * LINES : (j + 1) * LINES, :]
        coef_ref[0:R, :] = particles(gathered_ref).astype(bf16).T
        minus = lax.broadcasted_iota(jnp.int32, (R, NPART), 0) < 3
        coef_ref[R : 2 * R, :] = jnp.where(minus, -1.0, 0.0).astype(bf16)
        rows = []
        for s in range(SNAP):
            j = picks_ref[s]
            rows.append(gathered_ref[j // NP_DEV, pl.ds(j % NP_DEV, 1), :])
        rows.append(jnp.zeros((SNAP, R), f32))
        pick_ref[...] = jnp.concatenate(rows, axis=0).astype(bf16)

    for c in range(block // chunk):
        at = pl.ds(c * chunk, chunk)
        rows = basis_ref[at, :]
        columns = rows.T
        observed = obs_ref[:, at]
        left_ref[:, at] = (columns.astype(f32) * prec_ref[:, at]).astype(bf16)
        picked = jnp.dot(pick_ref[...], columns, preferred_element_type=f32)[0:SNAP]
        slopes = jnp.tanh(picked - observed)
        bend = (1.0 - slopes * slopes).astype(bf16)
        terms = jnp.concatenate([*in_three(observed), jnp.zeros((13, chunk), f32)], axis=0).astype(bf16)
        terms = jnp.concatenate([terms, jnp.zeros((R - 16, chunk), bf16)], axis=0).T
        field = jnp.dot(jnp.concatenate([rows, terms], axis=1), coef_ref[...], preferred_element_type=f32)
        right_ref[at, 0:NPART] = jnp.tanh(field).astype(bf16)
        for s in range(SNAP):
            first = NPART + s * R
            right_ref[at, first : first + R] = (bend[s : s + 1, :] * columns).T
    sums_ref[...] += jnp.dot(left_ref[...], right_ref[...], preferred_element_type=f32)

    @pl.when(step == pl.num_programs(0) - 1)
    def _():
        for core in range(2):

            @pl.when(lax.axis_index(C) == core)
            def _():
                for half, part_ref in ((core, keep_ref), (1 - core, send_ref)):
                    for k in range(HALF // R):
                        first = half * HALF + k * R
                        part_ref[k * R : (k + 1) * R, :] = sums_ref[:, first : first + R]


def in_hbm(x):
    return pltpu.with_memory_space_constraint(x, pltpu.HBM)


def points_pass(snapshots, pairs, observed, precision, basis):
    block, chunk = 4096, 256
    count = basis.shape[0]
    whole = lambda i, *_: (0, 0)
    return pl.pallas_call(
        functools.partial(points_kernel, block, chunk),
        out_shape=[jax.ShapeDtypeStruct((N_DOM, LINES, R), f32)] + [jax.ShapeDtypeStruct((HALF, R), f32)] * 2,
        grid_spec=pltpu.PrefetchScalarGridSpec(
            num_scalar_prefetch=1,
            grid=(count // block,),
            in_specs=[
                *[pl.BlockSpec((2 * LINES, R), whole)] * 4,
                pl.BlockSpec((1, block), lambda i, *_: (0, i)),
                pl.BlockSpec((1, block), lambda i, *_: (0, i)),
                pl.BlockSpec((block, R), lambda i, *_: (i, 0)),
            ],
            out_specs=[pl.BlockSpec((N_DOM, LINES, R), lambda i, *_: (0, 0, 0))] + [pl.BlockSpec((HALF, R), whole)] * 2,
            scratch_shapes=[
                pltpu.VMEM((2 * R, NPART), bf16),
                pltpu.VMEM((16, R), bf16),
                pltpu.VMEM((R, ROWS), f32),
                pltpu.VMEM((R, block), bf16),
                pltpu.VMEM((block, ROWS), bf16),
            ],
        ),
        compiler_params=pltpu.CompilerParams(vmem_limit_bytes=POINTS_VMEM),
        name="points_pass",
    )(in_hbm(snapshots), *pairs, *[in_hbm(a.reshape(1, count)) for a in (observed, precision)], basis)


def tile_at(n):
    return pl.ds(pl.multiple_of(n * 8, 8), 8)


def factor_and_solve(sys_ref, panel_ref, wide_ref, rhs_ref, out_ref):
    tiles = R // 8
    sub = lax.broadcasted_iota(jnp.int32, (8, R), 0)

    def row_of(ref, k, row):
        return jnp.broadcast_to(ref[k, pl.ds(row, 1), :], (8, R))

    def in_one_tile(rows):
        out = rows[0]
        for k in range(1, 8):
            out = jnp.where(sub == k, rows[k], out)
        return out

    def panel(p, base):
        first = p * 8
        corner = [[row_of(sys_ref, first + k, first + i) if i >= k else None for k in range(8)] for i in range(8)]
        low = [[None] * 8 for _ in range(8)]
        inverse = [None] * 8
        for k in range(8):
            inverse[k] = 1.0 / corner[k][k]
            for i in range(k + 1, 8):
                low[i][k] = corner[i][k] * inverse[k]
            for j in range(k + 1, 8):
                for i in range(j, 8):
                    corner[i][j] = corner[i][j] - corner[i][k] * low[j][k]
        y = [jnp.broadcast_to(rhs_ref[pl.ds(first + k, 1), :], (8, R)) for k in range(8)]
        for k in range(8):
            for m in range(k):
                y[k] = y[k] - low[k][m] * y[m]
        out_ref[tile_at(p), :] = in_one_tile([y[k] * inverse[k] for k in range(8)])

        def below(t, carry):
            at = tile_at(t)
            columns = [sys_ref[first + k, at, :] for k in range(8)]
            rhs = rhs_ref[at, :]
            for k in range(8):
                for m in range(k):
                    columns[k] = columns[k] - columns[m] * low[k][m]
                panel_ref[base + k, at, :] = columns[k]
                factor = columns[k] * inverse[k]
                sys_ref[first + k, at, :] = factor
                for r in range(8):
                    wide_ref[t * 8 + r, base + k] = jnp.broadcast_to(factor[r : r + 1], (8, R))
                rhs = rhs - factor * y[k]
            rhs_ref[at, :] = rhs
            return carry

        lax.fori_loop(p, tiles, below, 0)

    def update(depth, size, tj, start, h, carry):
        at = [tile_at(start + size * h + e) for e in range(size)]
        for j in range(8):
            row = tj * 8 + j
            total = [sys_ref[row, at[e], :] for e in range(size)]
            for k in range(depth):
                factor = wide_ref[row, k]
                for e in range(size):
                    total[e] = total[e] - panel_ref[k, at[e], :] * factor
            for e in range(size):
                sys_ref[row, at[e], :] = total[e]
        return carry

    def two_panels(q, carry):
        p = 2 * q
        panel(p, 0)
        lax.fori_loop(p + 1, tiles, functools.partial(update, 8, 1, p + 1, 0), 0)
        panel(p + 1, 8)

        def trailing(tj, carry):
            odd = (tiles - tj) % 2
            lax.fori_loop(0, odd, functools.partial(update, 16, 1, tj, tj), carry)
            return lax.fori_loop(0, (tiles - tj) // 2, functools.partial(update, 16, 2, tj, tj + odd), carry)

        return lax.fori_loop(p + 2, tiles, trailing, carry)

    lax.fori_loop(0, tiles // 2, two_panels, 0)

    def back(n, carry):
        p = tiles - 1 - n
        first = p * 8

        def gather(t, sums):
            at = tile_at(t)
            x = out_ref[at, :]
            return tuple(sums[k] + sys_ref[first + k, at, :] * x for k in range(8))

        sums = lax.fori_loop(p + 1, tiles, gather, tuple(jnp.zeros((8, R), f32) for _ in range(8)))
        x = [
            jnp.broadcast_to(out_ref[pl.ds(first + k, 1), :] - jnp.sum(sums[k], axis=0, keepdims=True), (8, R))
            for k in range(8)
        ]
        for k in range(7, 0, -1):
            for m in range(k):
                x[m] = x[m] - row_of(sys_ref, first + m, first + k) * x[k]
        out_ref[tile_at(p), :] = in_one_tile(x)
        return carry

    lax.fori_loop(0, tiles, back, 0)


def steps_kernel(picks_ref, gathered_ref, mine_ref, other_ref, out_ref,
                 sums_ref, sys_ref, panel_ref, wide_ref, rhs_ref, step_ref):
    scale = R / PTS
    core, dom = lax.axis_index(C), lax.axis_index(DOM)
    for half in range(2):

        @pl.when(core == half)
        def _():
            sums_ref[half * HALF : (half + 1) * HALF, :] = mine_ref[...]
            sums_ref[(1 - half) * HALF : (2 - half) * HALF, :] = other_ref[...]

    lane = lax.broadcasted_iota(jnp.int32, (8, R), 1)
    sub = lax.broadcasted_iota(jnp.int32, (8, R), 0)
    square_r = lax.broadcasted_iota(jnp.int32, (R, R), 0)
    square_q = lax.broadcasted_iota(jnp.int32, (R, R), 1)
    eye = (square_r == square_q).astype(f32)

    everyone = particles(gathered_ref)
    tags = [gathered_ref[d, NP_DEV : NP_DEV + 1, :] for d in range(N_DOM)]
    first_half = lane[0:1] < NP_DEV
    counts = jnp.concatenate(
        [jnp.where(first_half, tags[d], pltpu.roll(tags[d + 1], NP_DEV, 1)) for d in range(0, N_DOM, 2)], axis=1
    )

    owners = pltpu.roll(jnp.concatenate(tags, axis=0), NP_DEV, 1)
    named = jnp.where((owners == dom.astype(f32)) & (lane < NP_DEV), 1.0, 0.0)
    before = jnp.dot(named, (square_r < square_q).astype(f32), precision=highest, preferred_element_type=f32)
    slot = lax.broadcasted_iota(jnp.int32, (16, R), 0).astype(f32)
    own, valid = [], []
    for d in range(N_DOM):
        choose = jnp.where((named[d : d + 1] > 0.5) & (before[d : d + 1] == slot), 1.0, 0.0)
        valid.append(jnp.sum(choose, axis=1, keepdims=True))
        own.append(jnp.dot(choose[:, :NP_DEV], gathered_ref[d, 0:NP_DEV, :], precision=highest,
                           preferred_element_type=f32))
    own, valid = jnp.concatenate(own, axis=0), jnp.concatenate(valid, axis=0)

    mean_hess = sums_ref[NPART : NPART + R, :]
    for s in range(1, SNAP):
        mean_hess = mean_hess + sums_ref[NPART + s * R : NPART + (s + 1) * R, :]
    mean_hess = eye + mean_hess * (scale / SNAP)
    trace = jnp.sum(jnp.sum(mean_hess * eye, axis=1, keepdims=True), axis=0, keepdims=True)
    repulse = 6.0 / trace

    lifted = jnp.dot(everyone, mean_hess, precision=highest, preferred_element_type=f32)
    ones = jnp.ones((8, R), f32)
    norms = lax.dot_general(ones, lifted * everyone, last_pair, precision=highest, preferred_element_type=f32)[0:1]
    own_lift = jnp.dot(own, mean_hess, precision=highest, preferred_element_type=f32)
    own_norm = jnp.sum(own_lift * own, axis=1, keepdims=True)
    cross = lax.dot_general(own_lift, everyone, last_pair, precision=highest, preferred_element_type=f32)
    distance = own_norm + norms - 2.0 * cross
    weights = counts * jnp.exp(-3.0 * distance / trace)
    total = jnp.sum(weights, axis=1, keepdims=True)
    low_weights = weights.astype(bf16)
    carried = (everyone + repulse * lifted).astype(bf16)
    numerator = jnp.dot(low_weights, carried, preferred_element_type=f32)
    rounded = low_weights.astype(f32)
    grad = jnp.zeros((R, R), f32)
    for k in range(0, NPART, R):
        grad = grad + lax.dot_general(rounded[:, k : k + R], sums_ref[k : k + R, :], last_pair, precision=highest,
                                      preferred_element_type=f32)
    drift = -(numerator + scale * grad) / total + repulse * own_lift
    rhs_ref[...] = drift.T

    rows = []
    for s in range(SNAP):
        j = picks_ref[s]
        rows.append(gathered_ref[j // NP_DEV, pl.ds(j % NP_DEV, 1), :])
    rows.append(jnp.zeros((R - SNAP, R), f32))
    picked = jnp.concatenate(rows, axis=0)
    picked_lift = jnp.dot(picked, mean_hess, precision=highest, preferred_element_type=f32)
    picked_norm = lax.dot_general(ones, picked_lift * picked, last_pair, precision=highest,
                                  preferred_element_type=f32)[0:1]
    picked_cross = lax.dot_general(own_lift, picked, last_pair, precision=highest, preferred_element_type=f32)
    apart = 1.0 + (own_norm + picked_norm - 2.0 * picked_cross) / trace
    mixture = jnp.where(square_q < SNAP, 1.0 / (apart * apart), 0.0)
    mixture = mixture / jnp.sum(mixture, axis=1, keepdims=True)
    shares = mixture.T[0:SNAP, :]
    share_sum = jnp.sum(shares, axis=0, keepdims=True)
    high, middle, low = in_three(shares * scale)
    factors = jnp.concatenate([high, middle, low, high, middle, high], axis=0).astype(bf16)

    def assemble(g, carry):
        parts = []
        for k in range(8):
            hess_rows = sums_ref[pl.ds(NPART + g * 8 + k, SNAP, stride=R), :]
            high, middle, low = in_three(hess_rows)
            parts.append(jnp.concatenate([high, high, high, middle, middle, low], axis=0).astype(bf16))
        product = lax.dot_general(jnp.concatenate(parts, axis=1), factors, (((0,), (0,)), ((), ())),
                                  preferred_element_type=f32)
        for k in range(8):
            sys_ref[g * 8 + k] = product[k * R : (k + 1) * R]
            sys_ref[g * 8 + k, tile_at(g), :] += jnp.where(sub == k, share_sum, 0.0)
        return carry

    lax.fori_loop(0, R // 8, assemble, 0, unroll=8)
    factor_and_solve(sys_ref, panel_ref, wide_ref, rhs_ref, step_ref)
    out_ref[...] = jnp.where(valid > 0.5, own + step_ref[...].T, 0.0)


def newton_rows(snapshots, gathered, mine, other):
    vmem = pl.BlockSpec(memory_space=pltpu.VMEM)
    smem = pl.BlockSpec(memory_space=pltpu.SMEM)
    return pl.pallas_call(
        steps_kernel,
        out_shape=jax.ShapeDtypeStruct((R, R), f32),
        in_specs=[smem, vmem, vmem, vmem],
        out_specs=vmem,
        scratch_shapes=[
            pltpu.VMEM((ROWS + R, R), f32),
            pltpu.VMEM((R, R, R), f32),
            pltpu.VMEM((16, R, R), f32),
            pltpu.VMEM((R, 16, 8, R), f32),
            pltpu.VMEM((R, R), f32),
            pltpu.VMEM((R, R), f32),
        ],
        compiler_params=pltpu.CompilerParams(vmem_limit_bytes=STEPS_VMEM),
        name="newton_rows",
    )(snapshots, gathered, mine, other)


def sent_to_all(shard, axes):
    copies = jnp.broadcast_to(shard, (lax.axis_size(axes), *shard.shape))
    return lax.all_to_all(copies, axes, split_axis=0, concat_axis=0, tiled=True)


def body(coefficients, copies, owner, snapshots, basis, observed, precision):
    swap = [(0, 1), (1, 0)]
    lines = packed_lines(coefficients, copies, owner)
    pair = lax.all_gather(lines, C, axis=0, tiled=True)
    pairs = [pair] + [lax.ppermute(pair, Y, [(y, (y + shift) % 4) for y in range(4)]) for shift in (1, 3, 2)]
    gathered, keep, send = points_pass(snapshots, pairs, observed, precision, basis)
    part = keep + lax.ppermute(send, C, swap)
    chips = lax.axis_size(CHIPS)
    blocks = lax.all_to_all(part.reshape(chips, HALF // chips, R), CHIPS, 0, 0, tiled=True)
    mine = sent_to_all(jnp.sum(blocks, axis=0), CHIPS).reshape(HALF, R)
    other = lax.ppermute(mine, C, swap)
    rows = newton_rows(snapshots, gathered, mine, other)
    return rows.reshape(1, N_DOM, 2 * NP_DEV // N_DOM, R)


def solution(mesh):
    finer = Mesh(mesh.devices.reshape(4, 4, 4, 2), FIELD_DOM)
    return jax.shard_map(
        body,
        mesh=finer,
        in_specs=(
            P(DOM, None),
            P(DOM),
            P(DOM, None),
            P(),
            P(FIELD_DOM, None),
            P(FIELD_DOM),
            P(FIELD_DOM),
        ),
        out_specs=P(DOM, None, None, None),
        check_vma=False,
    )
```
